32 devices in a mesh: gx: 4 (over z), gy: 2 (over y), gz: 4 (over x, core).
Axes of the slice: x: 2, y: 2, z: 4, core: 2. Of those that a mesh axis runs over, the one named last changes fastest.
Arguments:
- saved: float32 [3, 27, 32, 16, 512], P(None, None, 'gx', 'gy', 'gz'), may hold values from 0.02 to 0.08
- porosity: float32 [32, 16, 512], P('gx', 'gy', 'gz'), may hold values from 0.05 to 0.6
- fluid: int32 [32, 16, 512], P('gx', 'gy', 'gz'), may hold values 0 or 1
- seed_adjoint: float32 [27, 32, 16, 512], P(None, 'gx', 'gy', 'gz'), may hold values from -6 to 6
Outputs:
- adjoint_first: float32 [27, 32, 16, 512], P(None, 'gx', 'gy', 'gz')
- porosity_grad: float32 [32, 16, 512], P('gx', 'gy', 'gz')
The draws below stay inside these ranges and needn't reach their ends.
All inputs are finite; a program needn't handle non-finite values. No bound on the sum of `fluid` on one device may be relied on, other than what follows from the above.
Results may differ from the reference program's by a relative error of at most 0.0001.
Values sent between devices are 32-bit elements; how exact they have to be, the bound alone decides.
No kernel may reach another device: no remote copies, remote signals or barrier semaphores. Data moves between devices by JAX's collectives and lax.ppermute only.
A program may use at most 64 MiB of HBM per device.

```python
import jax
import jax.numpy as jnp
import numpy as np
from jax import lax

Q = 27
STEPS = 3
NX = 32
NY = 16
NZ = 512


def plant(result, own_key, low, largest):
    longest = result.shape.index(max(result.shape))
    spots = []
    for shift in (0, 1):
        where = [jax.random.randint(jax.random.fold_in(own_key, axis), (), 0, length) for axis, length in enumerate(result.shape)]
        where[longest] = (where[longest] + shift) % result.shape[longest]
        spots.append(tuple(where))
    return result.at[spots[0]].set(low).at[spots[1]].set(largest)


def level_of(key, extent, split, smallest, largest):
    loudness, own = 1.0, jax.random.fold_in(key, 6)
    for position, blocks in split:
        heights = jnp.exp(jax.random.uniform(jax.random.fold_in(own, position), (blocks,), jnp.float32, smallest / len(split), largest / len(split)))
        loudness = loudness * jnp.repeat(heights, extent[position] // blocks).reshape([-1 if axis == position else 1 for axis in range(len(extent))])
    return loudness


def normal_values(own_key, extent, scale, reach, cuts=(), kind=jnp.bfloat16):
    drawn = scale * jax.random.normal(own_key, extent, jnp.float32)
    if cuts:
        drawn = drawn * level_of(own_key, extent, cuts, -0.22, 0.18)
    return jnp.clip(drawn, -reach, reach).astype(kind)


def setup_inputs(seed: int = 0) -> dict:
    arg_keys = jax.random.split(jax.random.key(seed), 5)
    saved = jnp.clip(0.02 + 0.06 * jax.random.uniform(arg_keys[0], (STEPS, Q, NX, NY, NZ), jnp.float32) ** level_of(arg_keys[0], (STEPS, Q, NX, NY, NZ), ((2, 4), (3, 2), (4, 4)), -0.2, 0.2), 0.02, 0.08)
    porosity = jnp.clip(0.05 + 0.55 * jax.random.uniform(arg_keys[1], (NX, NY, NZ), jnp.float32) ** level_of(arg_keys[1], (NX, NY, NZ), ((0, 4), (1, 2), (2, 4)), -0.2, 0.2), 0.05, 0.6)
    fluid = plant((jax.random.randint(arg_keys[2], (NX, NY, NZ), 0, 8) < 7).astype(jnp.int32), jax.random.fold_in(arg_keys[2], 1), 0, 1)
    seed_adjoint = normal_values(arg_keys[3], (Q, NX, NY, NZ), 1.0, 6.0, ((1, 4), (2, 2), (3, 4)), jnp.float32)
    return dict(saved=saved, porosity=porosity, fluid=fluid, seed_adjoint=seed_adjoint)


def lattice():
    vel = np.array([[a, b, c] for a in (-1, 0, 1) for b in (-1, 0, 1) for c in (-1, 0, 1)], dtype=np.int64)
    nonzero = np.abs(vel).sum(axis=1)
    table = np.array([8.0 / 27, 2.0 / 27, 1.0 / 54, 1.0 / 216])
    return (vel, table[nonzero])

def collide(pops, porosity, fluid):
    vel, weights = lattice()
    shape = (27, 1, 1, 1)
    vx = jnp.asarray(vel[:, 0].reshape(shape), jnp.float32)
    vy = jnp.asarray(vel[:, 1].reshape(shape), jnp.float32)
    vz = jnp.asarray(vel[:, 2].reshape(shape), jnp.float32)
    wts = jnp.asarray(weights.reshape(shape), jnp.float32)
    solid = jnp.where(fluid == 1, porosity, jnp.ones_like(porosity))
    density = lax.optimization_barrier(jnp.sum(pops, axis=0))
    ux = lax.optimization_barrier(jnp.sum(pops * vx, axis=0)) / density
    uy = lax.optimization_barrier(jnp.sum(pops * vy, axis=0)) / density
    uz = lax.optimization_barrier(jnp.sum(pops * vz, axis=0)) / density
    cu = vx * ux + vy * uy + vz * uz
    usq = ux * ux + uy * uy + uz * uz
    equil = wts * density * (1.0 + 3.0 * cu + 4.5 * cu * cu - 1.5 * usq)
    relaxed = pops - 1.6 * (pops - equil)
    return (1.0 - solid) * relaxed + solid * pops[::-1]

def pull(adjoint):
    vel, weights = lattice()
    nx, ny, nz = (adjoint.shape[1], adjoint.shape[2], adjoint.shape[3])
    padded = jnp.pad(adjoint, ((0, 0), (1, 1), (1, 1), (1, 1)))
    pieces = []
    for index in range(27):
        ax, ay, az = (int(vel[index, 0]) + 1, int(vel[index, 1]) + 1, int(vel[index, 2]) + 1)
        pieces.append(padded[index, ax:ax + nx, ay:ay + ny, az:az + nz])
    return jnp.stack(pieces, axis=0)

def reference(saved, porosity, fluid, seed_adjoint):
    adjoint = seed_adjoint
    grad = jnp.zeros(porosity.shape, jnp.float32)
    for step in range(STEPS - 1, -1, -1):
        pulled = pull(adjoint)
        outputs, backward = jax.vjp(lambda pops, poro: collide(pops, poro, fluid), saved[step], porosity)
        adjoint, term = backward(pulled)
        grad = grad + term
    return (adjoint, grad)
```

```python
import jax
import jax.numpy as jnp
import numpy as np
from jax import lax
from jax.sharding import PartitionSpec as P

STEPS = 3


def swapped(value, axis, odd, spare):
    length = lax.axis_size(axis)
    wide = lax.axis_size(spare) if spare else 1
    pairs = []
    for i in range(length):
        for k in range(wide):
            j, m = ((i + 1 if i % 2 == 1 else i - 1) if odd else i ^ 1), k
            if not 0 <= j < length:
                j, m = (i, k ^ 1) if spare else (j % length, k)
            if j < length and m < wide:
                pairs.append((i * wide + k, j * wide + m))
    return lax.ppermute(value, (axis, spare) if spare else axis, pairs)


def exchanged(to_lower, to_upper, axis, spare):
    length = lax.axis_size(axis)
    index = lax.axis_index(axis)
    even = index % 2 == 0
    first = swapped(jnp.where(even, to_upper, to_lower), axis, False, spare)
    if length > 2:
        second = swapped(jnp.where(even, to_lower, to_upper), axis, True, spare)
    else:
        second = jnp.zeros_like(first)
    zero = jnp.zeros_like(first)
    from_upper = jnp.where(index == length - 1, zero, jnp.where(even, first, second))
    from_lower = jnp.where(index == 0, zero, jnp.where(even, second, first))
    return (from_upper, from_lower)


def lattice():
    vel = np.array(
        [[a, b, c] for a in (-1, 0, 1) for b in (-1, 0, 1) for c in (-1, 0, 1)], dtype=np.int64
    )
    nonzero = np.abs(vel).sum(axis=1)
    table = np.array([8.0 / 27, 2.0 / 27, 1.0 / 54, 1.0 / 216])
    return (vel, table[nonzero])


def collide(pops, porosity, fluid):
    vel, weights = lattice()
    shape = (27, 1, 1, 1)
    vx = jnp.asarray(vel[:, 0].reshape(shape), jnp.float32)
    vy = jnp.asarray(vel[:, 1].reshape(shape), jnp.float32)
    vz = jnp.asarray(vel[:, 2].reshape(shape), jnp.float32)
    wts = jnp.asarray(weights.reshape(shape), jnp.float32)
    solid = jnp.where(fluid == 1, porosity, jnp.ones_like(porosity))
    density = jnp.sum(pops, axis=0)
    ux = jnp.sum(pops * vx, axis=0) / density
    uy = jnp.sum(pops * vy, axis=0) / density
    uz = jnp.sum(pops * vz, axis=0) / density
    cu = vx * ux + vy * uy + vz * uz
    usq = ux * ux + uy * uy + uz * uz
    equil = wts * density * (1.0 + 3.0 * cu + 4.5 * cu * cu - 1.5 * usq)
    relaxed = pops - 1.6 * (pops - equil)
    return (1.0 - solid) * relaxed + solid * pops[::-1]


def edge_planes(field, dim):
    first = jax.lax.slice_in_dim(field, 0, 1, axis=dim)
    last = jax.lax.slice_in_dim(field, field.shape[dim] - 1, field.shape[dim], axis=dim)
    return (first, last)


def move_along(adjoint, dim):
    vel, weights = lattice()
    column = vel[:, dim - 1]
    upward = [k for k in range(27) if int(column[k]) == 1]
    downward = [k for k in range(27) if int(column[k]) == -1]
    going_up = jnp.stack([adjoint[k] for k in upward], axis=0)
    going_down = jnp.stack([adjoint[k] for k in downward], axis=0)
    first, unused_last = edge_planes(going_up, dim)
    unused_first, last = edge_planes(going_down, dim)
    axis, spare = {1: ("gx", "gz"), 2: ("gy", "gz"), 3: ("gz", None)}[dim]
    from_upper, from_lower = exchanged(first, last, axis, spare)
    length = adjoint.shape[dim]
    moved_up = jnp.concatenate(
        [jax.lax.slice_in_dim(going_up, 1, length, axis=dim), from_upper], axis=dim
    )
    moved_down = jnp.concatenate(
        [from_lower, jax.lax.slice_in_dim(going_down, 0, length - 1, axis=dim)], axis=dim
    )
    pieces = []
    for index in range(27):
        if int(column[index]) == 1:
            pieces.append(moved_up[upward.index(index)])
        elif int(column[index]) == -1:
            pieces.append(moved_down[downward.index(index)])
        else:
            pieces.append(adjoint[index])
    return jnp.stack(pieces, axis=0)


def local(saved, porosity, fluid, seed_adjoint):
    adjoint = seed_adjoint
    grad = jnp.zeros(porosity.shape, jnp.float32)
    for step in range(STEPS - 1, -1, -1):
        pulled = move_along(move_along(move_along(adjoint, 1), 2), 3)
        outputs, backward = jax.vjp(
            lambda pops, poro: collide(pops, poro, fluid), saved[step], porosity
        )
        adjoint, term = backward(pulled)
        grad = grad + term
    return (adjoint, grad)


def solution(mesh):
    return jax.shard_map(
        local,
        mesh=mesh,
        in_specs=(
            P(None, None, "gx", "gy", "gz"),
            P("gx", "gy", "gz"),
            P("gx", "gy", "gz"),
            P(None, "gx", "gy", "gz"),
        ),
        out_specs=(P(None, "gx", "gy", "gz"), P("gx", "gy", "gz")),
        check_vma=False,
    )
```

```python
import functools

import jax
import jax.numpy as jnp
import numpy as np
from jax import lax
from jax.experimental import pallas as pl
from jax.experimental.pallas import tpu as pltpu
from jax.sharding import PartitionSpec as P

STEPS = 3
DEPTH = STEPS
SLOTS = 8
Q = 27

VEL = np.array([[a, b, c] for a in (-1, 0, 1) for b in (-1, 0, 1) for c in (-1, 0, 1)])


def pop(cx, cy, cz):
    return 9 * (cx + 1) + 3 * (cy + 1) + cz + 1


U2, U1, SOLID, FLUIDITY = 27, 30, 33, 34
TRAVEL = 34


def reach(quantity, dim, toward):
    if quantity < Q:
        return DEPTH - 1 - int(VEL[quantity, dim]) * toward
    return 1 if U1 <= quantity < U1 + 3 else 2


def mirrored(quantity, dim):
    if quantity >= Q:
        return quantity
    c = [int(v) for v in VEL[quantity]]
    c[dim] = -c[dim]
    return pop(*c)


UPWARD = [(q, p) for q in range(TRAVEL) for p in range(1, reach(q, 0, 1) + 1)]


def swapped(value, axis, odd, spare):
    length = lax.axis_size(axis)
    wide = lax.axis_size(spare) if spare else 1
    pairs = []
    for i in range(length):
        for k in range(wide):
            j, m = ((i + 1 if i % 2 == 1 else i - 1) if odd else i ^ 1), k
            if not 0 <= j < length:
                j, m = (i, k ^ 1) if spare else (j % length, k)
            if j < length and m < wide:
                pairs.append((i * wide + k, j * wide + m))
    return lax.ppermute(value, (axis, spare) if spare else axis, pairs)


def both_matchings(first, second, axis, spare):
    a = swapped(first, axis, False, spare)
    return a, (swapped(second, axis, True, spare) if lax.axis_size(axis) > 2 else a)


class Place:
    def __init__(self, axis):
        index = lax.axis_index(axis)
        self.even = lax.rem(index, 2) == 0
        self.lower = index > 0
        self.upper = index < lax.axis_size(axis) - 1

    def send(self, up, down):
        return jnp.where(self.even, up, down), jnp.where(self.even, down, up)

    def take(self, first, second):
        below = jnp.where(self.even, second, first)
        above = jnp.where(self.even, first, second)
        zero = jnp.zeros_like(first)
        return jnp.where(self.lower, below, zero), jnp.where(self.upper, above, zero)


class Shape:
    def __init__(self, nx, ny, nz):
        self.nx, self.ny, self.nz = nx, ny, nz
        self.rows = 2 * 8 * -(-(nx + 2 * DEPTH + 1) // 16)
        self.halo = nx + 2 * DEPTH
        if self.halo * SLOTS > nz or nx * SLOTS * 2 > nz or nx < DEPTH or ny != 8 or nz < 6:
            raise ValueError("local block")

    def at(self, quantity, row):
        start = (quantity * self.rows + row) * self.ny
        if not isinstance(start, int):
            start = pl.multiple_of(start, self.ny)
        return pl.ds(start, self.ny)

    def raw(self, quantity, x):
        start = (quantity * self.nx + x) * self.ny
        if not isinstance(start, int):
            start = pl.multiple_of(start, self.ny)
        return pl.ds(start, self.ny)

    def tile(self, index):
        return pl.ds(index * self.ny, self.ny)


def lanes(g):
    return lax.broadcasted_iota(jnp.int32, (g.ny, g.nz), 1)


def roll(value, by, axis):
    size = value.shape[axis]
    if isinstance(by, int):
        by = by % size
        if by == 0:
            return value
    return pltpu.roll(value, by, axis)


def moments(load):
    total, my, mz, sums = [], [], [], {}
    for a in (-1, 0, 1):
        t, z = [], []
        for b in (-1, 0, 1):
            low, mid, high = (load(pop(a, b, c)) for c in (-1, 0, 1))
            t.append(low + mid + high)
            z.append(high - low)
        total.append(t[0] + t[1] + t[2])
        my.append(t[2] - t[0])
        mz.append(z[0] + z[1] + z[2])
    return (
        total[0] + total[1] + total[2],
        total[2] - total[0],
        my[0] + my[1] + my[2],
        mz[0] + mz[1] + mz[2],
    )


def velocity(load):
    rho, mx, my, mz = moments(load)
    inverse = 1.0 / rho
    return rho, mx * inverse, my * inverse, mz * inverse


def open_kernel(g, seed, saved, porosity, fluid, za, zb, xa, xb, mom):
    nx = g.nx

    def row(x, carry):
        here = pl.ds(pl.multiple_of(x * g.ny, g.ny), g.ny)
        mom[g.raw(8, x), :] = jnp.where(fluid[here, :] == 1, porosity[here, :], 1.0)
        for step, base in ((2, 0), (1, 4)):
            found = velocity(lambda i: saved[g.raw(step * Q + i, x), :])
            for k in range(4):
                mom[g.raw(base + k, x), :] = found[k]
        return carry

    lax.fori_loop(0, nx, row, 0)

    def source(q, x):
        if q < Q:
            return seed[g.raw(q, x), :]
        return mom[g.raw({U2: 1, U1: 5, SOLID: 8}[q - q % 3 if q < SOLID else q] + (q % 3 if q < SOLID else 0), x), :]

    lane = lanes(g)
    group, offset = lane // SLOTS, lane % SLOTS
    joint = []
    for q in range(TRAVEL):
        half = (q % 2) * nx
        acc = joint.pop() if q % 2 else jnp.zeros((g.ny, g.nz), jnp.float32)
        for x in range(nx):
            moved = roll(source(q, x), (half + x) * SLOTS + DEPTH, 1)
            acc = jnp.where(group == half + x, moved, acc)
        joint.append(acc)
    z = Place("gz")
    if len(joint) % 2:
        joint.append(joint[-1])
    for k in range(len(joint) // 2):
        first, second = joint[2 * k], joint[2 * k + 1]
        up = jnp.where(offset < 4, first, roll(second, 4, 1))
        down = jnp.where(offset < 4, roll(first, -3, 1), roll(second, 1, 1))
        za[g.tile(k), :], zb[g.tile(k), :] = z.send(up, down)

    x = Place("gx")
    for k, (q, p) in enumerate(UPWARD):
        xa[g.tile(k), :], xb[g.tile(k), :] = x.send(source(q, nx - p), source(mirrored(q, 0), p - 1))


def swap_edges(g, field, i, row):
    lane = lanes(g)
    cz = int(VEL[i, 2])
    if cz == 0:
        return
    own, edge, slot = field[g.at(i, row), :], field[g.at(i, g.halo), :], row * SLOTS
    if cz > 0:
        here, out, back = 0, slot + DEPTH + 2, slot + DEPTH
    else:
        here, out, back = g.nz - 1, slot + DEPTH - 1, slot + DEPTH + 1
    field[g.at(i, row), :] = jnp.where(lane == here, roll(edge, here - out + g.nz, 1), own)
    field[g.at(i, g.halo), :] = jnp.where(lane == back, roll(own, back - here + g.nz, 1), edge)


def second_kernel(g, seed, mom, za, zb, sa, sb, field, extra):
    nx = g.nx
    lane = lanes(g)
    group, offset = lane // SLOTS, lane % SLOTS
    inner = (group >= DEPTH) & (group < DEPTH + nx)
    z = Place("gz")

    def target(q):
        return (field, q) if q < Q else (extra, q - Q)

    below, above = [], []
    for k in range(-(-TRAVEL // 4)):
        low, high = z.take(za[g.tile(k), :], zb[g.tile(k), :])
        below.append(low)
        above.append(high)
    halo = []
    for q in range(TRAVEL):
        at = (q % 2) * nx * SLOTS + (q // 2 % 2) * 4
        low = roll(below[q // 4], DEPTH * SLOTS - at, 1)
        high = roll(above[q // 4], DEPTH * SLOTS + DEPTH + 2 - at, 1)
        tile = jnp.where(offset < 4, low, high)
        halo.append(jnp.where(inner, tile, 0.0))
        ref, index = target(q)
        ref[g.at(index, g.halo), :] = halo[-1]
    x = Place("gx")
    width = DEPTH * SLOTS
    per = g.nz // width
    for k in range(-(-TRAVEL // per)):
        up = down = jnp.zeros((g.ny, g.nz), jnp.float32)
        for j in range(min(per, TRAVEL - k * per)):
            tile = halo[k * per + j]
            part = (lane >= j * width) & (lane < (j + 1) * width)
            up = jnp.where(part, roll(tile, j * width - nx * SLOTS, 1), up)
            down = jnp.where(part, roll(tile, j * width - DEPTH * SLOTS, 1), down)
        sa[g.tile(k), :], sb[g.tile(k), :] = x.send(up, down)

    def row(r, carry):
        for i in range(Q):
            field[g.at(i, r + DEPTH), :] = seed[g.raw(i, r), :]
            swap_edges(g, field, i, r + DEPTH)
        for k in range(3):
            extra[g.at(k, r + DEPTH), :] = mom[g.raw(1 + k, r), :]
            extra[g.at(3 + k, r + DEPTH), :] = mom[g.raw(5 + k, r), :]
        solid = mom[g.raw(8, r), :]
        extra[g.at(6, r + DEPTH), :] = solid
        extra[g.at(7, r + DEPTH), :] = 1.0 - solid
        return carry

    lax.fori_loop(0, nx, row, 0)


def y_message(g, field, ya, yb):
    y = Place("gy")
    for k in range(9):
        a, c = k // 3 - 1, k % 3 - 1
        for half in range(g.rows // 8):
            def line(i, edge):
                return field[pl.ds((i * g.rows + half * 8) * g.ny + edge, 8, stride=g.ny), :]
            here = pl.ds(k * g.rows + half * 8, 8)
            ya[here, :], yb[here, :] = y.send(line(pop(a, -1, c), g.ny - 1), line(pop(a, 1, c), 0))


def third_kernel(g, field, extra, xa, xb, sa, sb, field_out, extra_out, ya, yb):
    del field, extra
    nx = g.nx
    x, z = Place("gx"), Place("gz")
    lane = lanes(g)
    group, offset = lane // SLOTS, lane % SLOTS

    def target(q):
        return (field_out, q) if q < Q else (extra_out, q - Q)

    for k, (q, p) in enumerate(UPWARD):
        low, high = x.take(xa[g.tile(k), :], xb[g.tile(k), :])
        ref, index = target(q)
        ref[g.at(index, DEPTH - p), :] = low
        ref, index = target(mirrored(q, 0))
        ref[g.at(index, DEPTH + nx - 1 + p), :] = high
        if q == SOLID:
            extra_out[g.at(7, DEPTH - p), :] = jnp.where(x.lower, 1.0 - low, 0.0)
            extra_out[g.at(7, DEPTH + nx - 1 + p), :] = jnp.where(x.upper, 1.0 - high, 0.0)
    width = DEPTH * SLOTS
    per = g.nz // width
    for k in range(-(-TRAVEL // per)):
        low, high = x.take(sa[g.tile(k), :], sb[g.tile(k), :])
        for j in range(min(per, TRAVEL - k * per)):
            ref, index = target(k * per + j)
            tile = ref[g.at(index, g.halo), :]
            tile = jnp.where(group < DEPTH, roll(low, -j * width, 1), tile)
            tile = jnp.where(group >= DEPTH + nx, roll(high, (DEPTH + nx) * SLOTS - j * width, 1), tile)
            ref[g.at(index, g.halo), :] = tile
    there = jnp.where(group < DEPTH, jnp.where(x.lower, 1, 0), jnp.where(group >= DEPTH + nx, jnp.where(x.upper, 1, 0), 1))
    there = there * jnp.where(offset < 4, jnp.where(z.lower, 1, 0), jnp.where(z.upper, 1, 0))
    extra_out[g.at(7, g.halo), :] = jnp.where(there == 1, 1.0 - extra_out[g.at(6, g.halo), :], 0.0)

    for side in (0, DEPTH + nx):
        for i in range(Q):
            for r in range(side, side + DEPTH):
                swap_edges(g, field_out, i, r)
    y_message(g, field_out, ya, yb)


def pulled_moments(p):
    t = {}
    for a in (-1, 0, 1):
        s0, s1, s2 = [], [], []
        for b in (-1, 0, 1):
            low, mid, high = (p[pop(a, b, c)] for c in (-1, 0, 1))
            both = low + high
            s0.append(4.0 * mid + both)
            s1.append(high - low)
            s2.append(both)
        both = s0[0] + s0[2]
        t[a] = (
            4.0 * s0[1] + both,
            s0[2] - s0[0],
            both,
            4.0 * s1[1] + (s1[0] + s1[2]),
            s1[2] - s1[0],
            4.0 * s2[1] + (s2[0] + s2[2]),
        )
    both = [t[-1][k] + t[1][k] for k in range(6)]
    full = [4.0 * t[0][k] + both[k] for k in range(6)]
    m0, my, myy, mz, myz, mzz = full
    mx, mxx = t[1][0] - t[-1][0], both[0]
    mxy, mxz = t[1][1] - t[-1][1], t[1][3] - t[-1][3]
    return m0, mx, my, mz, mxx, myy, mzz, mxy, mxz, myz


def transposed(p, u, solid, fluidity):
    m0, mx, my, mz, mxx, myy, mzz, mxy, mxz, myz = pulled_moments(p)
    ux, uy, uz = u
    usq = ux * ux + uy * uy + uz * uz
    vx = mxx * ux + mxy * uy + mxz * uz
    vy = mxy * ux + myy * uy + myz * uz
    vz = mxz * ux + myz * uy + mzz * uz
    quad = ux * vx + uy * vy + uz * vz
    scale = fluidity * (1.6 / 216.0)
    kept = -0.6 * fluidity
    base = scale * (m0 + 1.5 * usq * m0 - 4.5 * quad)
    bx = scale * (3.0 * (mx - ux * m0) + 9.0 * vx)
    by = scale * (3.0 * (my - uy * m0) + 9.0 * vy)
    bz = scale * (3.0 * (mz - uz * m0) + 9.0 * vz)
    out = [None] * Q
    for a in (-1, 0, 1):
        ga = base + bx if a > 0 else (base - bx if a < 0 else base)
        for b in (-1, 0, 1):
            gb = ga + by if b > 0 else (ga - by if b < 0 else ga)
            for c in (-1, 0, 1):
                gc = gb + bz if c > 0 else (gb - bz if c < 0 else gb)
                i = pop(a, b, c)
                out[i] = kept * p[i] + solid * p[Q - 1 - i] + gc
    flow = m0 * (1.0 - 1.5 * usq) + 3.0 * (ux * mx + uy * my + uz * mz) + 4.5 * quad
    return out, flow


def step_kernel(g, step, field, extra, mom, saved, fluid, ya, yb, grad, kept, result, grad_out, *messages):
    del field
    nx = g.nx
    y = Place("gy")
    for k in range(9):
        a, c = k // 3 - 1, k % 3 - 1
        for half in range(g.rows // 8):
            here = pl.ds(k * g.rows + half * 8, 8)
            low, high = y.take(ya[here, :], yb[here, :])
            for i, edge, value in ((pop(a, -1, c), g.ny - 1, low), (pop(a, 1, c), 0, high)):
                kept[pl.ds((i * g.rows + half * 8) * g.ny + edge, 8, stride=g.ny), :] = value

    base = {2: 0, 1: 3, 0: None}[step]

    def parts(row):
        solid, fluidity = extra[g.at(6, row), :], extra[g.at(7, row), :]
        return tuple(extra[g.at(base + k, row), :] for k in range(3)), solid, fluidity

    if step:
        tile = [kept[g.at(i, g.halo), :] for i in range(Q)]
        p = [
            roll(roll(tile[i], -(SLOTS * int(VEL[i, 0]) + int(VEL[i, 2])), 1), -int(VEL[i, 1]), 0)
            for i in range(Q)
        ]
        out, _ = transposed(p, *parts(g.halo))
        for i in range(Q):
            result[g.at(i, g.halo), :] = out[i]

    def pull(row):
        return [
            roll(
                roll(kept[g.at(i, row + int(VEL[i, 0])), :], -int(VEL[i, 2]), 1),
                -int(VEL[i, 1]),
                0,
            )
            for i in range(Q)
        ]

    def store(row, out):
        for i in range(Q):
            result[g.at(i, row), :] = out[i]
            swap_edges(g, result, i, row)

    def outer(row):
        out, _ = transposed(pull(row), *parts(row))
        store(row, out)

    def inner(x, carry):
        row = x + DEPTH
        here = pl.ds(pl.multiple_of(x * g.ny, g.ny), g.ny)
        p = pull(row)
        if step:
            u, solid, fluidity = parts(row)
            rho = mom[g.raw(4 * (2 - step), x), :]
        else:
            rho, *u = velocity(lambda i: saved[g.raw(i, x), :])
            solid, fluidity = extra[g.at(6, row), :], extra[g.at(7, row), :]
        out, flow = transposed(p, u, solid, fluidity)
        same = cross = None
        for i in range(Q):
            f = saved[g.raw(step * Q + i, x), :]
            one, two = p[i] * f, p[Q - 1 - i] * f
            same, cross = (one, two) if same is None else (same + one, cross + two)
        term = 0.6 * same + cross - (1.6 / 216.0) * (rho * flow)
        grad_out[here, :] = jnp.where(fluid[here, :] == 1, grad[here, :] + term, 0.0)
        if step:
            store(row, out)
        else:
            for i in range(Q):
                result[g.raw(i, x), :] = out[i]
        return carry

    lax.fori_loop(0, nx, inner, 0)
    if step:
        for r in range(DEPTH - step + 1 - 1, DEPTH):
            if r >= STEPS - step:
                outer(r)
        for r in range(DEPTH + nx, DEPTH + nx + step):
            if r < DEPTH + nx + step - 0:
                outer(r)
        y_message(g, result, *messages)


def call(kernel, name, outs, args, flops, aliases=None):
    moved = 4 * sum(int(np.prod(a.shape)) for a in [*args, *outs])
    return pl.pallas_call(
        kernel,
        name=name,
        out_shape=[jax.ShapeDtypeStruct(o, jnp.float32) if isinstance(o, tuple) else o for o in outs],
        in_specs=[pl.BlockSpec(memory_space=pltpu.VMEM)] * len(args),
        out_specs=[pl.BlockSpec(memory_space=pltpu.VMEM)] * len(outs),
        input_output_aliases=aliases or {},
        compiler_params=pltpu.CompilerParams(vmem_limit_bytes=VMEM_LIMIT),
        cost_estimate=pl.CostEstimate(flops=flops, bytes_accessed=moved, transcendentals=0),
    )(*args)


VMEM_LIMIT = 24 * 1024 * 1024


def local(saved, porosity, fluid, seed_adjoint):
    nx, ny, nz = porosity.shape
    g = Shape(nx, ny, nz)
    f32 = lambda *shape: jax.ShapeDtypeStruct(shape, jnp.float32)
    seed = seed_adjoint.reshape(Q * nx * ny, nz)
    pops = saved.reshape(STEPS * Q * nx * ny, nz)
    porosity = porosity.reshape(nx * ny, nz)
    fluid = fluid.reshape(nx * ny, nz)
    voxels = nx * ny * nz

    zs = f32(-(-TRAVEL // 4) * ny, nz)
    xs = f32(len(UPWARD) * ny, nz)
    za, zb, xa, xb, mom = call(
        functools.partial(open_kernel, g), "open", [zs, zs, xs, xs, f32(9 * nx * ny, nz)],
        [seed, pops, porosity, fluid], 200 * voxels,
    )
    za, zb = both_matchings(za, zb, "gz", None)
    xa, xb = both_matchings(xa, xb, "gx", "gz")
    per = nz // (DEPTH * SLOTS)
    ss = f32(-(-TRAVEL // per) * ny, nz)
    whole, more = f32(Q * g.rows * ny, nz), f32(8 * g.rows * ny, nz)
    sa, sb, field, extra = call(
        functools.partial(second_kernel, g), "second", [ss, ss, whole, more], [seed, mom, za, zb], 100 * voxels
    )
    sa, sb = both_matchings(sa, sb, "gx", "gz")
    ys = f32(9 * g.rows, nz)
    field, extra, ya, yb = call(
        functools.partial(third_kernel, g), "third", [whole, more, ys, ys],
        [field, extra, xa, xb, sa, sb], 100 * voxels, {0: 0, 1: 1},
    )
    grad = jnp.zeros((nx * ny, nz), jnp.float32)
    flat = f32(nx * ny, nz)
    for step in (2, 1):
        ya, yb = both_matchings(ya, yb, "gy", "gz")
        _, field, grad, ya, yb = call(
            functools.partial(step_kernel, g, step), f"step{step}", [whole, whole, flat, ys, ys],
            [field, extra, mom, pops, fluid, ya, yb, grad], 400 * voxels, {0: 0},
        )
    ya, yb = both_matchings(ya, yb, "gy", "gz")
    _, adjoint, grad = call(
        functools.partial(step_kernel, g, 0), "step0", [whole, f32(Q * nx * ny, nz), flat],
        [field, extra, mom, pops, fluid, ya, yb, grad], 400 * voxels, {0: 0},
    )
    return adjoint.reshape(Q, nx, ny, nz), grad.reshape(nx, ny, nz)


def solution(mesh):
    return jax.shard_map(
        local,
        mesh=mesh,
        in_specs=(
            P(None, None, "gx", "gy", "gz"),
            P("gx", "gy", "gz"),
            P("gx", "gy", "gz"),
            P(None, "gx", "gy", "gz"),
        ),
        out_specs=(P(None, "gx", "gy", "gz"), P("gx", "gy", "gz")),
        check_vma=False,
    )
```

```python
import functools

import jax
import jax.numpy as jnp
import numpy as np
from jax import lax
from jax.experimental import pallas as pl
from jax.experimental.pallas import tpu as pltpu
from jax.sharding import PartitionSpec as P

STEPS = 3
DEPTH = STEPS
SLOTS = 8
Q = 27

VEL = np.array([[a, b, c] for a in (-1, 0, 1) for b in (-1, 0, 1) for c in (-1, 0, 1)])


def pop(cx, cy, cz):
    return 9 * (cx + 1) + 3 * (cy + 1) + cz + 1


U2, U1, SOLID, FLUIDITY = 27, 30, 33, 34
TRAVEL = 34


def reach(quantity, dim, toward):
    if quantity < Q:
        return DEPTH - 1 - int(VEL[quantity, dim]) * toward
    return 1 if U1 <= quantity < U1 + 3 else 2


def mirrored(quantity, dim):
    if quantity >= Q:
        return quantity
    c = [int(v) for v in VEL[quantity]]
    c[dim] = -c[dim]
    return pop(*c)


UPWARD = [(q, p) for q in range(TRAVEL) for p in range(1, reach(q, 0, 1) + 1)]


def swapped(value, axis, odd, spare):
    length = lax.axis_size(axis)
    wide = lax.axis_size(spare) if spare else 1
    pairs = []
    for i in range(length):
        for k in range(wide):
            j, m = ((i + 1 if i % 2 == 1 else i - 1) if odd else i ^ 1), k
            if not 0 <= j < length:
                j, m = (i, k ^ 1) if spare else (j % length, k)
            if j < length and m < wide:
                pairs.append((i * wide + k, j * wide + m))
    return lax.ppermute(value, (axis, spare) if spare else axis, pairs)


def both_matchings(first, second, axis, spare):
    a = swapped(first, axis, False, spare)
    return a, (swapped(second, axis, True, spare) if lax.axis_size(axis) > 2 else a)


class Place:
    def __init__(self, axis):
        index = lax.axis_index(axis)
        self.even = lax.rem(index, 2) == 0
        self.lower = index > 0
        self.upper = index < lax.axis_size(axis) - 1

    def send(self, up, down):
        return jnp.where(self.even, up, down), jnp.where(self.even, down, up)

    def take(self, first, second):
        below = jnp.where(self.even, second, first)
        above = jnp.where(self.even, first, second)
        zero = jnp.zeros_like(first)
        return jnp.where(self.lower, below, zero), jnp.where(self.upper, above, zero)


class Shape:
    def __init__(self, nx, ny, nz):
        self.nx, self.ny, self.nz = nx, ny, nz
        self.rows = 2 * 8 * -(-(nx + 2 * DEPTH + 1) // 16)
        self.halo = nx + 2 * DEPTH
        if self.halo * SLOTS > nz or nx * SLOTS * 2 > nz or nx < DEPTH or ny != 8 or nz < 6:
            raise ValueError("local block")

    def at(self, quantity, row):
        start = (quantity * self.rows + row) * self.ny
        if not isinstance(start, int):
            start = pl.multiple_of(start, self.ny)
        return pl.ds(start, self.ny)

    def raw(self, quantity, x):
        start = (quantity * self.nx + x) * self.ny
        if not isinstance(start, int):
            start = pl.multiple_of(start, self.ny)
        return pl.ds(start, self.ny)

    def tile(self, index):
        return pl.ds(index * self.ny, self.ny)


def lanes(g):
    return lax.broadcasted_iota(jnp.int32, (g.ny, g.nz), 1)


def roll(value, by, axis):
    size = value.shape[axis]
    if isinstance(by, int):
        by = by % size
        if by == 0:
            return value
    return pltpu.roll(value, by, axis)


def moments(load):
    total, my, mz, sums = [], [], [], {}
    for a in (-1, 0, 1):
        t, z = [], []
        for b in (-1, 0, 1):
            low, mid, high = (load(pop(a, b, c)) for c in (-1, 0, 1))
            t.append(low + mid + high)
            z.append(high - low)
        total.append(t[0] + t[1] + t[2])
        my.append(t[2] - t[0])
        mz.append(z[0] + z[1] + z[2])
    return (
        total[0] + total[1] + total[2],
        total[2] - total[0],
        my[0] + my[1] + my[2],
        mz[0] + mz[1] + mz[2],
    )


def velocity(load):
    rho, mx, my, mz = moments(load)
    inverse = 1.0 / rho
    return rho, mx * inverse, my * inverse, mz * inverse


def open_kernel(g, seed, saved, porosity, fluid, za, zb, xa, xb, mom):
    nx = g.nx

    def row(x, carry):
        here = pl.ds(pl.multiple_of(x * g.ny, g.ny), g.ny)
        mom[g.raw(8, x), :] = jnp.where(fluid[here, :] == 1, porosity[here, :], 1.0)
        for step, base in ((2, 0), (1, 4)):
            found = velocity(lambda i: saved[g.raw(step * Q + i, x), :])
            for k in range(4):
                mom[g.raw(base + k, x), :] = found[k]
        return carry

    lax.fori_loop(0, nx, row, 0)

    def source(q, x):
        if q < Q:
            return seed[g.raw(q, x), :]
        return mom[g.raw({0: 1, 1: 5, 2: 8}[(q - Q) // 3] + (q - Q) % 3, x), :]

    lane = lanes(g)
    group, offset = lane // SLOTS, lane % SLOTS
    joint = []
    for q in range(TRAVEL):
        half = (q % 2) * nx
        acc = joint.pop() if q % 2 else jnp.zeros((g.ny, g.nz), jnp.float32)
        for x in range(nx):
            moved = roll(source(q, x), (half + x) * SLOTS + DEPTH, 1)
            acc = jnp.where(group == half + x, moved, acc)
        joint.append(acc)
    z = Place("gz")
    if len(joint) % 2:
        joint.append(joint[-1])
    for k in range(len(joint) // 2):
        first, second = joint[2 * k], joint[2 * k + 1]
        up = jnp.where(offset < 4, first, roll(second, 4, 1))
        down = jnp.where(offset < 4, roll(first, -3, 1), roll(second, 1, 1))
        za[g.tile(k), :], zb[g.tile(k), :] = z.send(up, down)

    x = Place("gx")
    for k, (q, p) in enumerate(UPWARD):
        xa[g.tile(k), :], xb[g.tile(k), :] = x.send(source(q, nx - p), source(mirrored(q, 0), p - 1))


def swap_edges(g, field, i, row):
    lane = lanes(g)
    cz = int(VEL[i, 2])
    if cz == 0:
        return
    own, edge, slot = field[g.at(i, row), :], field[g.at(i, g.halo), :], row * SLOTS
    if cz > 0:
        here, out, back = 0, slot + DEPTH + 2, slot + DEPTH
    else:
        here, out, back = g.nz - 1, slot + DEPTH - 1, slot + DEPTH + 1
    field[g.at(i, row), :] = jnp.where(lane == here, roll(edge, here - out + g.nz, 1), own)
    field[g.at(i, g.halo), :] = jnp.where(lane == back, roll(own, back - here + g.nz, 1), edge)


def second_kernel(g, seed, mom, za, zb, sa, sb, field, extra):
    nx = g.nx
    lane = lanes(g)
    group, offset = lane // SLOTS, lane % SLOTS
    inner = (group >= DEPTH) & (group < DEPTH + nx)
    z = Place("gz")

    def target(q):
        return (field, q) if q < Q else (extra, q - Q)

    below, above = [], []
    for k in range(-(-TRAVEL // 4)):
        low, high = z.take(za[g.tile(k), :], zb[g.tile(k), :])
        below.append(low)
        above.append(high)
    halo = []
    for q in range(TRAVEL):
        at = (q % 2) * nx * SLOTS + (q // 2 % 2) * 4
        low = roll(below[q // 4], DEPTH * SLOTS - at, 1)
        high = roll(above[q // 4], DEPTH * SLOTS + DEPTH + 2 - at, 1)
        tile = jnp.where(offset < 4, low, high)
        halo.append(jnp.where(inner, tile, 0.0))
        ref, index = target(q)
        ref[g.at(index, g.halo), :] = halo[-1]
    x = Place("gx")
    width = DEPTH * SLOTS
    per = g.nz // width
    for k in range(-(-TRAVEL // per)):
        up = down = jnp.zeros((g.ny, g.nz), jnp.float32)
        for j in range(min(per, TRAVEL - k * per)):
            tile = halo[k * per + j]
            part = (lane >= j * width) & (lane < (j + 1) * width)
            up = jnp.where(part, roll(tile, j * width - nx * SLOTS, 1), up)
            down = jnp.where(part, roll(tile, j * width - DEPTH * SLOTS, 1), down)
        sa[g.tile(k), :], sb[g.tile(k), :] = x.send(up, down)

    for r in range(nx):
        for i in range(Q):
            field[g.at(i, r + DEPTH), :] = seed[g.raw(i, r), :]
            swap_edges(g, field, i, r + DEPTH)
        for k in range(3):
            extra[g.at(k, r + DEPTH), :] = mom[g.raw(1 + k, r), :]
            extra[g.at(3 + k, r + DEPTH), :] = mom[g.raw(5 + k, r), :]
        solid = mom[g.raw(8, r), :]
        extra[g.at(6, r + DEPTH), :] = solid
        extra[g.at(7, r + DEPTH), :] = 1.0 - solid


def y_message(g, field, ya, yb):
    y = Place("gy")
    for k in range(9):
        a, c = k // 3 - 1, k % 3 - 1
        for half in range(g.rows // 8):
            def line(i, edge):
                return field[pl.ds((i * g.rows + half * 8) * g.ny + edge, 8, stride=g.ny), :]
            here = pl.ds(k * g.rows + half * 8, 8)
            ya[here, :], yb[here, :] = y.send(line(pop(a, -1, c), g.ny - 1), line(pop(a, 1, c), 0))


def third_kernel(g, field, extra, xa, xb, sa, sb, field_out, extra_out, ya, yb):
    del field, extra
    nx = g.nx
    x, z = Place("gx"), Place("gz")
    lane = lanes(g)
    group, offset = lane // SLOTS, lane % SLOTS

    def target(q):
        return (field_out, q) if q < Q else (extra_out, q - Q)

    for k, (q, p) in enumerate(UPWARD):
        low, high = x.take(xa[g.tile(k), :], xb[g.tile(k), :])
        ref, index = target(q)
        ref[g.at(index, DEPTH - p), :] = low
        ref, index = target(mirrored(q, 0))
        ref[g.at(index, DEPTH + nx - 1 + p), :] = high
        if q == SOLID:
            extra_out[g.at(7, DEPTH - p), :] = jnp.where(x.lower, 1.0 - low, 0.0)
            extra_out[g.at(7, DEPTH + nx - 1 + p), :] = jnp.where(x.upper, 1.0 - high, 0.0)
    width = DEPTH * SLOTS
    per = g.nz // width
    for k in range(-(-TRAVEL // per)):
        low, high = x.take(sa[g.tile(k), :], sb[g.tile(k), :])
        for j in range(min(per, TRAVEL - k * per)):
            ref, index = target(k * per + j)
            tile = ref[g.at(index, g.halo), :]
            tile = jnp.where(group < DEPTH, roll(low, -j * width, 1), tile)
            tile = jnp.where(group >= DEPTH + nx, roll(high, (DEPTH + nx) * SLOTS - j * width, 1), tile)
            ref[g.at(index, g.halo), :] = tile
    there = jnp.where(group < DEPTH, jnp.where(x.lower, 1, 0), jnp.where(group >= DEPTH + nx, jnp.where(x.upper, 1, 0), 1))
    there = there * jnp.where(offset < 4, jnp.where(z.lower, 1, 0), jnp.where(z.upper, 1, 0))
    extra_out[g.at(7, g.halo), :] = jnp.where(there == 1, 1.0 - extra_out[g.at(6, g.halo), :], 0.0)

    for side in (0, DEPTH + nx):
        for i in range(Q):
            for r in range(side, side + DEPTH):
                swap_edges(g, field_out, i, r)
    y_message(g, field_out, ya, yb)


def pulled_moments(p):
    t = {}
    for a in (-1, 0, 1):
        s0, s1, s2 = [], [], []
        for b in (-1, 0, 1):
            low, mid, high = (p[pop(a, b, c)] for c in (-1, 0, 1))
            both = low + high
            s0.append(4.0 * mid + both)
            s1.append(high - low)
            s2.append(both)
        both = s0[0] + s0[2]
        t[a] = (
            4.0 * s0[1] + both,
            s0[2] - s0[0],
            both,
            4.0 * s1[1] + (s1[0] + s1[2]),
            s1[2] - s1[0],
            4.0 * s2[1] + (s2[0] + s2[2]),
        )
    both = [t[-1][k] + t[1][k] for k in range(6)]
    full = [4.0 * t[0][k] + both[k] for k in range(6)]
    m0, my, myy, mz, myz, mzz = full
    mx, mxx = t[1][0] - t[-1][0], both[0]
    mxy, mxz = t[1][1] - t[-1][1], t[1][3] - t[-1][3]
    return m0, mx, my, mz, mxx, myy, mzz, mxy, mxz, myz


def transposed(p, u, solid, fluidity):
    m0, mx, my, mz, mxx, myy, mzz, mxy, mxz, myz = pulled_moments(p)
    ux, uy, uz = u
    usq = ux * ux + uy * uy + uz * uz
    vx = mxx * ux + mxy * uy + mxz * uz
    vy = mxy * ux + myy * uy + myz * uz
    vz = mxz * ux + myz * uy + mzz * uz
    quad = ux * vx + uy * vy + uz * vz
    scale = fluidity * (1.6 / 216.0)
    kept = -0.6 * fluidity
    base = scale * (m0 + 1.5 * usq * m0 - 4.5 * quad)
    bx = scale * (3.0 * (mx - ux * m0) + 9.0 * vx)
    by = scale * (3.0 * (my - uy * m0) + 9.0 * vy)
    bz = scale * (3.0 * (mz - uz * m0) + 9.0 * vz)
    out = [None] * Q
    for a in (-1, 0, 1):
        ga = base + bx if a > 0 else (base - bx if a < 0 else base)
        for b in (-1, 0, 1):
            gb = ga + by if b > 0 else (ga - by if b < 0 else ga)
            for c in (-1, 0, 1):
                gc = gb + bz if c > 0 else (gb - bz if c < 0 else gb)
                i = pop(a, b, c)
                out[i] = kept * p[i] + solid * p[Q - 1 - i] + gc
    flow = m0 * (1.0 - 1.5 * usq) + 3.0 * (ux * mx + uy * my + uz * mz) + 4.5 * quad
    return out, flow


def step_kernel(g, step, field, extra, mom, saved, fluid, ya, yb, grad, kept, result, grad_out, *messages):
    del field
    nx = g.nx
    y = Place("gy")
    for k in range(9):
        a, c = k // 3 - 1, k % 3 - 1
        for half in range(g.rows // 8):
            here = pl.ds(k * g.rows + half * 8, 8)
            low, high = y.take(ya[here, :], yb[here, :])
            for i, edge, value in ((pop(a, -1, c), g.ny - 1, low), (pop(a, 1, c), 0, high)):
                kept[pl.ds((i * g.rows + half * 8) * g.ny + edge, 8, stride=g.ny), :] = value

    base = {2: 0, 1: 3, 0: None}[step]

    def parts(row):
        solid, fluidity = extra[g.at(6, row), :], extra[g.at(7, row), :]
        return tuple(extra[g.at(base + k, row), :] for k in range(3)), solid, fluidity

    if step:
        tile = [kept[g.at(i, g.halo), :] for i in range(Q)]
        p = [
            roll(roll(tile[i], -(SLOTS * int(VEL[i, 0]) + int(VEL[i, 2])), 1), -int(VEL[i, 1]), 0)
            for i in range(Q)
        ]
        out, _ = transposed(p, *parts(g.halo))
        for i in range(Q):
            result[g.at(i, g.halo), :] = out[i]

    def pull(row):
        return [
            roll(
                roll(kept[g.at(i, row + int(VEL[i, 0])), :], -int(VEL[i, 2]), 1),
                -int(VEL[i, 1]),
                0,
            )
            for i in range(Q)
        ]

    def store(row, out):
        for i in range(Q):
            result[g.at(i, row), :] = out[i]
            swap_edges(g, result, i, row)

    def outer(row):
        out, _ = transposed(pull(row), *parts(row))
        store(row, out)

    def inner(x, carry):
        row = x + DEPTH
        here = g.tile(x) if step else pl.ds(pl.multiple_of(x * g.ny, g.ny), g.ny)
        p = pull(row)
        if step:
            u, solid, fluidity = parts(row)
            rho = mom[g.raw(4 * (2 - step), x), :]
        else:
            rho, *u = velocity(lambda i: saved[g.raw(i, x), :])
            solid, fluidity = extra[g.at(6, row), :], extra[g.at(7, row), :]
        out, flow = transposed(p, u, solid, fluidity)
        same = cross = None
        for i in range(Q):
            f = saved[g.raw(step * Q + i, x), :]
            one, two = p[i] * f, p[Q - 1 - i] * f
            same, cross = (one, two) if same is None else (same + one, cross + two)
        term = 0.6 * same + cross - (1.6 / 216.0) * (rho * flow)
        grad_out[here, :] = jnp.where(fluid[here, :] == 1, grad[here, :] + term, 0.0)
        if step:
            store(row, out)
        else:
            for i in range(Q):
                result[g.raw(i, x), :] = out[i]
        return carry

    if not step:
        lax.fori_loop(0, nx, inner, 0)
    else:
        for x in range(nx):
            inner(x, 0)
        for r in (*range(DEPTH - step, DEPTH), *range(DEPTH + nx, DEPTH + nx + step)):
            outer(r)
        y_message(g, result, *messages)


def call(kernel, name, outs, args, flops, aliases=None):
    moved = 4 * sum(int(np.prod(a.shape)) for a in [*args, *outs])
    return pl.pallas_call(
        kernel,
        name=name,
        out_shape=[jax.ShapeDtypeStruct(o, jnp.float32) if isinstance(o, tuple) else o for o in outs],
        in_specs=[pl.BlockSpec(memory_space=pltpu.VMEM)] * len(args),
        out_specs=[pl.BlockSpec(memory_space=pltpu.VMEM)] * len(outs),
        input_output_aliases=aliases or {},
        compiler_params=pltpu.CompilerParams(vmem_limit_bytes=VMEM_LIMIT),
        cost_estimate=pl.CostEstimate(flops=flops, bytes_accessed=moved, transcendentals=0),
    )(*args)


VMEM_LIMIT = 24 * 1024 * 1024


def local(saved, porosity, fluid, seed_adjoint):
    nx, ny, nz = porosity.shape
    g = Shape(nx, ny, nz)
    f32 = lambda *shape: jax.ShapeDtypeStruct(shape, jnp.float32)
    seed = seed_adjoint.reshape(Q * nx * ny, nz)
    pops = saved.reshape(STEPS * Q * nx * ny, nz)
    porosity = porosity.reshape(nx * ny, nz)
    fluid = fluid.reshape(nx * ny, nz)
    voxels = nx * ny * nz

    zs = f32(-(-TRAVEL // 4) * ny, nz)
    xs = f32(len(UPWARD) * ny, nz)
    za, zb, xa, xb, mom = call(
        functools.partial(open_kernel, g), "open", [zs, zs, xs, xs, f32(9 * nx * ny, nz)],
        [seed, pops, porosity, fluid], 200 * voxels,
    )
    za, zb = both_matchings(za, zb, "gz", None)
    xa, xb = both_matchings(xa, xb, "gx", "gz")
    per = nz // (DEPTH * SLOTS)
    ss = f32(-(-TRAVEL // per) * ny, nz)
    whole, more = f32(Q * g.rows * ny, nz), f32(8 * g.rows * ny, nz)
    sa, sb, field, extra = call(
        functools.partial(second_kernel, g), "second", [ss, ss, whole, more], [seed, mom, za, zb], 100 * voxels
    )
    sa, sb = both_matchings(sa, sb, "gx", "gz")
    ys = f32(9 * g.rows, nz)
    field, extra, ya, yb = call(
        functools.partial(third_kernel, g), "third", [whole, more, ys, ys],
        [field, extra, xa, xb, sa, sb], 100 * voxels, {0: 0, 1: 1},
    )
    grad = jnp.zeros((nx * ny, nz), jnp.float32)
    flat = f32(nx * ny, nz)
    for step in (2, 1):
        ya, yb = both_matchings(ya, yb, "gy", "gz")
        _, field, grad, ya, yb = call(
            functools.partial(step_kernel, g, step), f"step{step}", [whole, whole, flat, ys, ys],
            [field, extra, mom, pops, fluid, ya, yb, grad], 400 * voxels, {0: 0},
        )
    ya, yb = both_matchings(ya, yb, "gy", "gz")
    _, adjoint, grad = call(
        functools.partial(step_kernel, g, 0), "step0", [whole, f32(Q * nx * ny, nz), flat],
        [field, extra, mom, pops, fluid, ya, yb, grad], 400 * voxels, {0: 0},
    )
    return adjoint.reshape(Q, nx, ny, nz), grad.reshape(nx, ny, nz)


def solution(mesh):
    return jax.shard_map(
        local,
        mesh=mesh,
        in_specs=(
            P(None, None, "gx", "gy", "gz"),
            P("gx", "gy", "gz"),
            P("gx", "gy", "gz"),
            P(None, "gx", "gy", "gz"),
        ),
        out_specs=(P(None, "gx", "gy", "gz"), P("gx", "gy", "gz")),
        check_vma=False,
    )
```

```python
import functools

import jax
import jax.numpy as jnp
import numpy as np
from jax import lax
from jax.experimental import pallas as pl
from jax.experimental.pallas import tpu as pltpu
from jax.sharding import PartitionSpec as P

STEPS = 3
DEPTH = STEPS
SLOTS = 8
Q = 27

VEL = np.array([[a, b, c] for a in (-1, 0, 1) for b in (-1, 0, 1) for c in (-1, 0, 1)])


def pop(cx, cy, cz):
    return 9 * (cx + 1) + 3 * (cy + 1) + cz + 1


U2, U1, SOLID, FLUIDITY = 27, 30, 33, 34
TRAVEL = 34


def reach(quantity, dim, toward):
    if quantity < Q:
        return DEPTH - 1 - int(VEL[quantity, dim]) * toward
    return 1 if U1 <= quantity < U1 + 3 else 2


def mirrored(quantity, dim):
    if quantity >= Q:
        return quantity
    c = [int(v) for v in VEL[quantity]]
    c[dim] = -c[dim]
    return pop(*c)


UPWARD = [(q, p) for q in range(TRAVEL) for p in range(1, reach(q, 0, 1) + 1)]


def swapped(value, axis, odd, spare):
    length = lax.axis_size(axis)
    wide = lax.axis_size(spare) if spare else 1
    pairs = []
    for i in range(length):
        for k in range(wide):
            j, m = ((i + 1 if i % 2 == 1 else i - 1) if odd else i ^ 1), k
            if not 0 <= j < length:
                j, m = (i, k ^ 1) if spare else (j % length, k)
            if j < length and m < wide:
                pairs.append((i * wide + k, j * wide + m))
    return lax.ppermute(value, (axis, spare) if spare else axis, pairs)


def both_matchings(messages, axis, spare):
    return [swapped(m, axis, k == 1, spare) for k, m in enumerate(messages)]


def matchings(axis):
    return 2 if lax.axis_size(axis) > 2 else 1


class Place:
    def __init__(self, axis):
        index = lax.axis_index(axis)
        self.even = lax.rem(index, 2) == 0
        self.lower = index > 0
        self.upper = index < lax.axis_size(axis) - 1

    def send(self, up, down):
        return jnp.where(self.even, up, down), jnp.where(self.even, down, up)

    def put(self, refs, here, up, down):
        for ref, value in zip(refs, self.send(up, down)):
            ref[here, :] = value

    def take(self, refs, here):
        first, second = refs[0][here, :], refs[-1][here, :]
        below = jnp.where(self.even, second, first)
        above = jnp.where(self.even, first, second)
        zero = jnp.zeros_like(first)
        return jnp.where(self.lower, below, zero), jnp.where(self.upper, above, zero)


class Shape:
    def __init__(self, nx, ny, nz):
        self.nx, self.ny, self.nz = nx, ny, nz
        self.rows = nz // SLOTS
        self.halo = nx + DEPTH
        if nx + 2 * DEPTH >= self.rows or nx * SLOTS * 2 > nz or nx < DEPTH or ny != 8 or self.rows % 8:
            raise ValueError("local block")

    def row(self, x):
        return x % self.rows

    def at(self, quantity, row):
        return pl.ds((quantity * self.rows + row) * self.ny, self.ny)

    def line(self, quantity, y):
        return pl.ds(quantity * self.rows * self.ny + y, self.rows, stride=self.ny)

    def raw(self, quantity, x):
        start = (quantity * self.nx + x) * self.ny
        if not isinstance(start, int):
            start = pl.multiple_of(start, self.ny)
        return pl.ds(start, self.ny)

    def raw_line(self, quantity, y):
        return pl.ds(quantity * self.nx * self.ny + y, self.nx, stride=self.ny)

    def late(self, quantity, row):
        return pl.ds((quantity * (self.rows - self.nx) + row - self.nx) * self.ny, self.ny)

    def late_line(self, quantity, y):
        count = self.rows - self.nx
        return pl.ds(quantity * count * self.ny + y, count, stride=self.ny)

    def tile(self, index):
        return pl.ds(index * self.ny, self.ny)


def lanes(g):
    return lax.broadcasted_iota(jnp.int32, (g.ny, g.nz), 1)


def roll(value, by, axis):
    size = value.shape[axis]
    if isinstance(by, int):
        by = by % size
        if by == 0:
            return value
    return pltpu.roll(value, by, axis)


def moments(load):
    total, my, mz, sums = [], [], [], {}
    for a in (-1, 0, 1):
        t, z = [], []
        for b in (-1, 0, 1):
            low, mid, high = (load(pop(a, b, c)) for c in (-1, 0, 1))
            t.append(low + mid + high)
            z.append(high - low)
        total.append(t[0] + t[1] + t[2])
        my.append(t[2] - t[0])
        mz.append(z[0] + z[1] + z[2])
    return (
        total[0] + total[1] + total[2],
        total[2] - total[0],
        my[0] + my[1] + my[2],
        mz[0] + mz[1] + mz[2],
    )


def velocity(load):
    rho, mx, my, mz = moments(load)
    inverse = 1.0 / rho
    return rho, mx * inverse, my * inverse, mz * inverse


def source(g, seed, mom, q, x):
    if q < Q:
        return seed[g.raw(q, x), :]
    return mom[g.raw({0: 1, 1: 5, 2: 8}[(q - Q) // 3] + (q - Q) % 3, x), :]


def open_kernel(g, seed_in, saved_in, porosity_in, fluid_in, seed, mom, saved, fluid, *refs):
    nx = g.nx
    *messages, porosity, sems = refs
    block = Q * nx * g.ny
    copies = [
        pltpu.make_async_copy(seed_in, seed, sems.at[0]),
        pltpu.make_async_copy(porosity_in, porosity, sems.at[1]),
        pltpu.make_async_copy(fluid_in, fluid, sems.at[2]),
        pltpu.make_async_copy(saved_in.at[pl.ds(2 * block, block), :], saved.at[pl.ds(0, block), :], sems.at[3]),
        pltpu.make_async_copy(saved_in.at[pl.ds(block, block), :], saved.at[pl.ds(block, block), :], sems.at[4]),
    ]
    for copy in copies:
        copy.start()
    lane = lanes(g)
    group, offset = lane // SLOTS, lane % SLOTS
    joint = []
    for q in range(TRAVEL):
        if q == 0:
            copies[0].wait()
        if q == Q:
            for copy in copies[1:]:
                copy.wait()

            def row(x, carry):
                here = g.raw(0, x)
                mom[g.raw(8, x), :] = jnp.where(fluid[here, :] == 1, porosity[here, :], 1.0)
                for part in range(2):
                    found = velocity(lambda i: saved[g.raw(part * Q + i, x), :])
                    for k in range(4):
                        mom[g.raw(4 * part + k, x), :] = found[k]
                return carry

            lax.fori_loop(0, nx, row, 0)
        half = (q % 2) * nx
        acc = joint.pop() if q % 2 else jnp.zeros((g.ny, g.nz), jnp.float32)
        for x in range(nx):
            moved = roll(source(g, seed, mom, q, x), (half + x) * SLOTS + DEPTH, 1)
            acc = jnp.where(group == half + x, moved, acc)
        joint.append(acc)
    z = Place("gz")
    if len(joint) % 2:
        joint.append(joint[-1])
    for k in range(len(joint) // 2):
        first, second = joint[2 * k], joint[2 * k + 1]
        up = jnp.where(offset < 4, first, roll(second, 4, 1))
        down = jnp.where(offset < 4, roll(first, -3, 1), roll(second, 1, 1))
        z.put(messages, g.tile(k), up, down)


def bulk_kernel(g, seed, mom, *messages):
    x = Place("gx")
    for k, (q, p) in enumerate(UPWARD):
        up, down = source(g, seed, mom, q, g.nx - p), source(g, seed, mom, mirrored(q, 0), p - 1)
        x.put(messages, g.tile(k), up, down)


def place_kernel(g, mom, saved_in, extra, mom0, saved, sem):
    nx = g.nx
    fetch = pltpu.make_async_copy(saved_in.at[pl.ds(0, Q * nx * g.ny), :], saved, sem)
    fetch.start()
    for x in range(nx):
        for k in range(3):
            extra[g.raw(k, x), :] = mom[g.raw(1 + k, x), :]
            extra[g.raw(3 + k, x), :] = mom[g.raw(5 + k, x), :]
        solid = mom[g.raw(8, x), :]
        extra[g.raw(6, x), :] = solid
        extra[g.raw(7, x), :] = 1.0 - solid
    fetch.wait()

    def row(x, carry):
        found = velocity(lambda i: saved[g.raw(i, x), :])
        for k in range(4):
            mom0[g.raw(k, x), :] = found[k]
        return carry

    lax.fori_loop(0, nx, row, 0)


def swap_edges(g, i, row, own, edge):
    lane = lanes(g)
    cz = int(VEL[i, 2])
    if cz == 0:
        return own, edge
    slot = row * SLOTS
    if cz > 0:
        here, out, back = 0, slot + DEPTH + 2, slot + DEPTH
    else:
        here, out, back = g.nz - 1, slot + DEPTH - 1, slot + DEPTH + 1
    return (
        jnp.where(lane == here, roll(edge, here - out, 1), own),
        jnp.where(lane == back, roll(own, back - here, 1), edge),
    )


def second_kernel(g, *refs):
    nx = g.nx
    heard, halo, messages = refs[: matchings("gz")], refs[matchings("gz")], refs[matchings("gz") + 1 :]
    lane = lanes(g)
    group, offset = lane // SLOTS, lane % SLOTS
    z, x = Place("gz"), Place("gx")
    below, above = [], []
    for k in range(-(-TRAVEL // 4)):
        low, high = z.take(heard, g.tile(k))
        below.append(low)
        above.append(high)
    tiles = []
    for q in range(TRAVEL):
        at = (q % 2) * nx * SLOTS + (q // 2 % 2) * 4
        low = roll(below[q // 4], -at, 1)
        high = roll(above[q // 4], DEPTH + 2 - at, 1)
        tiles.append(jnp.where(group < nx, jnp.where(offset < 4, low, high), 0.0))
        halo[g.tile(q), :] = tiles[-1]
    width = DEPTH * SLOTS
    per = g.nz // width
    for k in range(-(-TRAVEL // per)):
        up = down = jnp.zeros((g.ny, g.nz), jnp.float32)
        for j in range(min(per, TRAVEL - k * per)):
            tile = tiles[k * per + j]
            part = (lane >= j * width) & (lane < (j + 1) * width)
            up = jnp.where(part, roll(tile, j * width - (nx - DEPTH) * SLOTS, 1), up)
            down = jnp.where(part, roll(tile, j * width, 1), down)
        x.put(messages, g.tile(k), up, down)


def edges_kernel(g, seed, halo, field, turned, up, down):
    for i in range(Q):
        edge = halo[g.tile(i), :]
        for x in range(g.nx):
            own, edge = swap_edges(g, i, x, seed[g.raw(i, x), :], edge)
            field[g.raw(i, x), :] = own
        turned[g.tile(i), :] = edge
    for k in range(9):
        a, c = k // 3 - 1, k % 3 - 1
        here = pl.ds(k * g.nx, g.nx)
        up[here, :] = field[g.raw_line(pop(a, -1, c), g.ny - 1), :]
        down[here, :] = field[g.raw_line(pop(a, 1, c), 0), :]


def rows_kernel(g, *refs):
    *heard, field, extra = refs
    x = Place("gx")
    for k, (q, p) in enumerate(UPWARD):
        low, high = x.take(heard, g.tile(k))
        for index, row, value, there in (
            (q, g.row(-p), low, x.lower),
            (mirrored(q, 0), g.row(g.nx - 1 + p), high, x.upper),
        ):
            if index < Q:
                field[g.late(index, row), :] = value
            else:
                extra[g.late(index - Q, row), :] = value
            if index == SOLID:
                extra[g.late(7, row), :] = jnp.where(there, 1.0 - value, 0.0)


def third_kernel(g, turned, halo, rows, extras, up, down, *refs):
    nx = g.nx
    heard, (field, extra, *messages) = refs[: matchings("gx")], refs[matchings("gx") :]
    x, y, z = Place("gx"), Place("gy"), Place("gz")
    lane = lanes(g)
    group, offset = lane // SLOTS, lane % SLOTS

    def target(q):
        return (field, q) if q < Q else (extra, q - Q)

    lower, upper = group >= g.rows - DEPTH, (group >= nx) & (group < nx + DEPTH)
    width = DEPTH * SLOTS
    per = g.nz // width
    edges = []
    for k in range(-(-TRAVEL // per)):
        low, high = x.take(heard, g.tile(k))
        for j in range(min(per, TRAVEL - k * per)):
            q = k * per + j
            tile = turned[g.tile(q), :] if q < Q else halo[g.tile(q), :]
            tile = jnp.where(lower, roll(low, (g.rows - DEPTH) * SLOTS - j * width, 1), tile)
            edges.append(jnp.where(upper, roll(high, nx * SLOTS - j * width, 1), tile))
    extra[...] = extras[...]
    for q in range(TRAVEL):
        ref, index = target(q)
        edge = edges[q]
        if q < Q:
            for p in range(1, DEPTH + 1):
                for row, toward in ((g.row(-p), 1), (nx - 1 + p, -1)):
                    if p > reach(q, 0, toward):
                        continue
                    own, edge = swap_edges(g, q, row, rows[g.late(q, row), :], edge)
                    field[g.late(q, row), :] = own
        ref[g.late(index, g.halo), :] = edge
    there = jnp.where(lower, jnp.where(x.lower, 1, 0), jnp.where(upper, jnp.where(x.upper, 1, 0), 1))
    there = there * jnp.where(offset < 4, jnp.where(z.lower, 1, 0), jnp.where(z.upper, 1, 0))
    extra[g.late(7, g.halo), :] = jnp.where(there == 1, 1.0 - edges[SOLID], 0.0)
    for k in range(9):
        a, c = k // 3 - 1, k % 3 - 1
        for late in (False, True):
            here = pl.ds(k * g.rows + late * nx, g.rows - nx if late else nx)
            if late:
                sent = field[g.late_line(pop(a, -1, c), g.ny - 1), :], field[g.late_line(pop(a, 1, c), 0), :]
            else:
                sent = up[pl.ds(k * nx, nx), :], down[pl.ds(k * nx, nx), :]
            y.put(messages, here, *sent)


def pulled_moments(p):
    t = {}
    for a in (-1, 0, 1):
        s0, s1, s2 = [], [], []
        for b in (-1, 0, 1):
            low, mid, high = (p[pop(a, b, c)] for c in (-1, 0, 1))
            both = low + high
            s0.append(4.0 * mid + both)
            s1.append(high - low)
            s2.append(both)
        both = s0[0] + s0[2]
        t[a] = (
            4.0 * s0[1] + both,
            s0[2] - s0[0],
            both,
            4.0 * s1[1] + (s1[0] + s1[2]),
            s1[2] - s1[0],
            4.0 * s2[1] + (s2[0] + s2[2]),
        )
    both = [t[-1][k] + t[1][k] for k in range(6)]
    full = [4.0 * t[0][k] + both[k] for k in range(6)]
    m0, my, myy, mz, myz, mzz = full
    mx, mxx = t[1][0] - t[-1][0], both[0]
    mxy, mxz = t[1][1] - t[-1][1], t[1][3] - t[-1][3]
    return m0, mx, my, mz, mxx, myy, mzz, mxy, mxz, myz


def edge_moments(p, side):
    t = {}
    for a in (-1, 0, 1):
        low, mid, high = (p[pop(a, side, c)] for c in (-1, 0, 1))
        both = low + high
        t[a] = (4.0 * mid + both, high - low, both)
    both = [t[-1][k] + t[1][k] for k in range(3)]
    m0, mz, mzz = (4.0 * t[0][k] + both[k] for k in range(3))
    mx, mxz = t[1][0] - t[-1][0], t[1][1] - t[-1][1]
    if side > 0:
        return m0, mx, m0, mz, both[0], m0, mzz, mx, mxz, mz
    return m0, mx, -m0, mz, both[0], m0, mzz, -mx, mxz, -mz


def transposed(p, u, solid, fluidity, side=0):
    found = edge_moments(p, side) if side else pulled_moments(p)
    m0, mx, my, mz, mxx, myy, mzz, mxy, mxz, myz = found
    ux, uy, uz = u
    usq = ux * ux + uy * uy + uz * uz
    vx = mxx * ux + mxy * uy + mxz * uz
    vy = mxy * ux + myy * uy + myz * uz
    vz = mxz * ux + myz * uy + mzz * uz
    quad = ux * vx + uy * vy + uz * vz
    scale = fluidity * (1.6 / 216.0)
    kept = -0.6 * fluidity
    base = scale * (m0 + 1.5 * usq * m0 - 4.5 * quad)
    bx = scale * (3.0 * (mx - ux * m0) + 9.0 * vx)
    by = scale * (3.0 * (my - uy * m0) + 9.0 * vy)
    bz = scale * (3.0 * (mz - uz * m0) + 9.0 * vz)
    out = [None] * Q
    for a in (-1, 0, 1):
        ga = base + bx if a > 0 else (base - bx if a < 0 else base)
        for b in (-1, 0, 1):
            gb = ga + by if b > 0 else (ga - by if b < 0 else ga)
            for c in (-1, 0, 1):
                gc = gb + bz if c > 0 else (gb - bz if c < 0 else gb)
                i = pop(a, b, c)
                if not side or b == side:
                    gc = kept * p[i] + gc
                if not side or b == -side:
                    gc = solid * p[Q - 1 - i] + gc
                out[i] = gc
    flow = m0 * (1.0 - 1.5 * usq) + 3.0 * (ux * mx + uy * my + uz * mz) + 4.5 * quad
    return out, flow


def inner_kernel(g, step, early, late, extra, extra_late, mom, saved, fluid, grad, *refs):
    nx = g.nx
    base, part_at = 3 * (2 - step), (Q if step == 1 else 0)
    lines = refs[:2] if step < STEPS - 1 else None
    *outs, field = refs[2:] if lines else refs
    zero = jnp.zeros((g.rows, g.nz), jnp.float32)
    for i in range(Q):
        for row in range(g.rows):
            field[g.at(i, row), :] = early[g.raw(i, row), :] if row < nx else late[g.late(i, row), :]
        if VEL[i, 1] < 0:
            field[g.line(i, g.ny - 1), :] = zero
        elif lines:
            field[g.line(i, g.ny - 1), :] = lines[0][pl.ds(i * g.rows, g.rows), :]
        if VEL[i, 1] > 0:
            field[g.line(i, 0), :] = zero
        elif lines:
            field[g.line(i, 0), :] = lines[1][pl.ds(i * g.rows, g.rows), :]

    def part(k, row):
        return extra[g.raw(k, row), :] if row < nx else extra_late[g.late(k, row), :]

    def parts(row):
        return [part(k, row) for k in (base, base + 1, base + 2, 6, 7)]

    def pull(row):
        return [
            roll(
                roll(field[g.at(i, g.row(row + int(VEL[i, 0]))), :], -int(VEL[i, 2]), 1),
                -int(VEL[i, 1]),
                0,
            )
            for i in range(Q)
        ]

    if step:
        next_early, next_late, grad_out = outs
        p = [
            roll(
                roll(field[g.at(i, g.halo), :], -(SLOTS * int(VEL[i, 0]) + int(VEL[i, 2])), 1),
                -int(VEL[i, 1]),
                0,
            )
            for i in range(Q)
        ]
        *u, solid, fluidity = parts(g.halo)
        out, _ = transposed(p, u, solid, fluidity)
        for i in range(Q):
            next_late[g.late(i, g.halo), :] = out[i]
    else:
        result, up, down, grad_out = outs

    for x in range(-step, nx + step):
        row, local = g.row(x), 0 <= x < nx
        p = pull(row)
        if step:
            *u, solid, fluidity = parts(row)
        else:
            u = [mom[g.raw(1 + k, x), :] for k in range(3)]
            solid, fluidity = part(6, row), part(7, row)
        out, flow = transposed(p, u, solid, fluidity)
        if local:
            rho = mom[g.raw(4 * (2 - step) if step else 0, x), :]
            same = cross = None
            for i in range(Q):
                f = saved[g.raw(part_at + i, x), :]
                one, two = p[i] * f, p[Q - 1 - i] * f
                same, cross = (one, two) if same is None else (same + one, cross + two)
            term = 0.6 * same + cross - (1.6 / 216.0) * (rho * flow)
            here = g.tile(x)
            grad_out[here, :] = jnp.where(fluid[here, :] == 1, grad[here, :] + term, 0.0)
        for i in range(Q):
            if step:
                here = g.late(i, g.halo)
                own, edge = swap_edges(g, i, row, out[i], next_late[here, :])
                if VEL[i, 2]:
                    next_late[here, :] = edge
                if row < nx:
                    next_early[g.raw(i, row), :] = own
                else:
                    next_late[g.late(i, row), :] = own
            else:
                result[g.raw(i, x), :] = out[i]
    if not step:
        for i in range(Q):
            here = pl.ds(i * nx, nx)
            up[here, :] = result[g.raw_line(i, g.ny - 1), :]
            down[here, :] = result[g.raw_line(i, 0), :]


def edge_kernel(g, step, sending, *refs):
    nx = g.nx
    y = Place("gy")
    base = 3 * (2 - step)
    sub = lax.broadcasted_iota(jnp.int32, (g.rows, g.nz), 0)
    lane = lax.broadcasted_iota(jnp.int32, (g.rows, g.nz), 1)
    part_at = Q if step == 1 else 0
    heard, refs = refs[: matchings("gy")], refs[matchings("gy") :]
    early, late, extra, extra_late, mom, *refs = refs
    if sending:
        *messages, up, down = refs
    elif step:
        saved, fluid, grad_in, up, down, grad = refs
    else:
        saved, fluid, grad_in, _, whole, grad, up, down, sems = refs
    if not sending:
        grad[...] = grad_in[...]

    def wanted(side):
        return [i for i in range(Q) if not sending or VEL[i, 1] == -side]

    def joined(first, second, k, edge):
        return jnp.concatenate([first[g.raw_line(k, edge), :], second[g.late_line(k, edge), :]], axis=0)

    def swapped_edges(i, tile):
        cz = int(VEL[i, 2])
        here, out, back = (0, DEPTH + 2, DEPTH) if cz > 0 else (g.nz - 1, DEPTH - 1, DEPTH + 1)
        own = jnp.broadcast_to(tile[:, here : here + 1], tile.shape)
        edge = jnp.broadcast_to(tile[g.halo : g.halo + 1, :], tile.shape)
        column = jnp.sum(jnp.where(lane == sub * SLOTS + out, edge, 0.0), axis=1, keepdims=True)
        line = jnp.sum(jnp.where(lane == sub * SLOTS + back, own, 0.0), axis=0, keepdims=True)
        tile = jnp.where((lane == here) & (sub != g.halo), column, tile)
        return jnp.where((sub == g.halo) & (lane % SLOTS == back), line, tile)

    def before(i, side):
        if step:
            return joined(early, late, i, g.ny - 1 if side > 0 else 0)
        return (early if side > 0 else late)[pl.ds(i * nx, nx), :]

    def store(side, i, value):
        count = g.rows if step else nx
        (up if side > 0 else down)[pl.ds(i * count, count), :] = value

    def correct(side):
        edge = g.ny - 1 if side > 0 else 0
        p = [None] * Q
        for k in range(9):
            a, c = k // 3 - 1, k % 3 - 1
            here = pl.ds(k * g.rows, g.rows)
            first, second = heard[0][here, :], heard[-1][here, :]
            value = jnp.where(y.even if side > 0 else jnp.logical_not(y.even), first, second)
            moved = roll(roll(value, -a, 0), -c, 1)
            if step:
                moved = jnp.where(sub == g.halo, roll(value, -(SLOTS * a + c), 1), moved)
            else:
                moved = moved[:nx]
            p[pop(a, side, c)] = moved
        if step:
            *u, solid, fluidity = (joined(extra, extra_late, k, edge) for k in (base, base + 1, base + 2, 6, 7))
        else:
            u = [mom[g.raw_line(1 + k, edge), :] for k in range(3)]
            solid, fluidity = (extra[g.raw_line(k, edge), :] for k in (6, 7))
        out, flow = transposed(p, u, solid, fluidity, side)
        for i in wanted(side):
            tile = swapped_edges(i, out[i]) if step and VEL[i, 2] else out[i]
            store(side, i, before(i, side) + tile)
        if sending:
            return
        rho = mom[g.raw_line(4 * (2 - step) if step else 0, edge), :]
        same = cross = None
        for i in range(Q):
            if VEL[i, 1] != side:
                continue
            value = p[i][:nx]
            one = value * saved[g.raw_line(part_at + i, edge), :]
            two = value * saved[g.raw_line(part_at + Q - 1 - i, edge), :]
            same, cross = (one, two) if same is None else (same + one, cross + two)
        term = 0.6 * same + cross - (1.6 / 216.0) * (rho * flow[:nx])
        at = g.raw_line(0, edge)
        grad[at, :] = jnp.where(fluid[at, :] == 1, grad_in[at, :] + term, 0.0)

    def write(side):
        edge = g.ny - 1 if side > 0 else 0
        return pltpu.make_async_copy(up if side > 0 else down, whole.at[:, edge, :], sems.at[0 if side > 0 else 1])

    for side, there in ((1, y.upper), (-1, y.lower)):

        @pl.when(there)
        def _(side=side):
            correct(side)
            if not step:
                write(side).start()

        if step:

            @pl.when(jnp.logical_not(there))
            def _(side=side):
                for i in wanted(side):
                    store(side, i, before(i, side))

    if sending:
        for k in range(9):
            a, c = k // 3 - 1, k % 3 - 1
            here = pl.ds(k * g.rows, g.rows)
            sent = (up, pop(a, -1, c)), (down, pop(a, 1, c))
            y.put(messages, here, *(ref[pl.ds(i * g.rows, g.rows), :] for ref, i in sent))
    elif not step:
        for side, there in ((1, y.upper), (-1, y.lower)):

            @pl.when(there)
            def _(side=side):
                write(side).wait()


def call(kernel, name, outs, args, flops, aliases=None, scratch=(), spaces=None, out_spaces=None):
    moved = 4 * sum(int(np.prod(a.shape)) for a in [*args, *outs])
    spaces = spaces or [pltpu.VMEM] * len(args)
    out_spaces = out_spaces or [pltpu.VMEM] * len(outs)
    return pl.pallas_call(
        kernel,
        name=name,
        out_shape=outs,
        in_specs=[pl.BlockSpec(memory_space=m) for m in spaces],
        out_specs=[pl.BlockSpec(memory_space=m) for m in out_spaces],
        scratch_shapes=scratch,
        input_output_aliases=aliases or {},
        compiler_params=pltpu.CompilerParams(vmem_limit_bytes=VMEM_LIMIT),
        cost_estimate=pl.CostEstimate(flops=flops, bytes_accessed=moved, transcendentals=0),
    )(*args)


VMEM_LIMIT = 24 * 1024 * 1024


def local(saved, porosity, fluid, seed_adjoint):
    nx, ny, nz = porosity.shape
    g = Shape(nx, ny, nz)
    bind = functools.partial
    f32 = lambda *shape: jax.ShapeDtypeStruct(shape, jnp.float32)
    seed = seed_adjoint.reshape(Q * nx * ny, nz)
    pops = saved.reshape(STEPS * Q * nx * ny, nz)
    porosity = porosity.reshape(nx * ny, nz)
    fluid = fluid.reshape(nx * ny, nz)
    voxels, rest = nx * ny * nz, (g.rows - nx) * ny
    flat, full, late = f32(nx * ny, nz), f32(Q * nx * ny, nz), f32(Q * rest, nz)
    zs = f32(-(-TRAVEL // 4) * ny, nz)
    xs = f32(len(UPWARD) * ny, nz)
    ss = f32(-(-TRAVEL // (nz // (DEPTH * SLOTS))) * ny, nz)
    ys, yl, lines = f32(9 * g.rows, nz), f32(9 * nx, nz), f32(Q * g.rows, nz)

    hbm = lambda *values: [pltpu.with_memory_space_constraint(v, pltpu.HBM) for v in values]
    nmx, nmy, nmz = (matchings(axis) for axis in ("gx", "gy", "gz"))
    seed, mom, late_pops, fluid, *zm = call(
        bind(open_kernel, g), "open",
        [full, f32(9 * nx * ny, nz), f32(2 * Q * nx * ny, nz), jax.ShapeDtypeStruct((nx * ny, nz), jnp.int32), *[zs] * nmz],
        hbm(seed, pops, porosity, fluid), 200 * voxels, spaces=[pltpu.HBM] * 4,
        scratch=[pltpu.VMEM((nx * ny, nz), jnp.float32), pltpu.SemaphoreType.DMA((5,))],
    )
    with jax.named_scope("zswap"):
        zm = both_matchings(zm, "gz", None)
    with jax.named_scope("bulk"):
        xm = call(bind(bulk_kernel, g), "bulk", [xs] * nmx, [seed, mom], 10 * voxels)
    with jax.named_scope("xswap"):
        xm = both_matchings(xm, "gx", "gz")
    extra, mom0, first_pops = call(
        bind(place_kernel, g), "place", [f32(8 * nx * ny, nz), f32(4 * nx * ny, nz), full],
        [mom, *hbm(pops)], 50 * voxels, spaces=[pltpu.VMEM, pltpu.HBM], scratch=[pltpu.SemaphoreType.DMA(())],
    )
    halo, *sm = call(bind(second_kernel, g), "second", [f32(TRAVEL * ny, nz), *[ss] * nmx], zm, 20 * voxels)
    with jax.named_scope("smallswap"):
        sm = both_matchings(sm, "gx", "gz")
    early, turned, up, down = call(
        bind(edges_kernel, g), "edges", [full, f32(Q * ny, nz), yl, yl], [seed, halo], 50 * voxels
    )
    rows, extra_rows = call(bind(rows_kernel, g), "rows", [late, f32(8 * rest, nz)], xm, 20 * voxels)
    late_rows, extra_late, *ym = call(
        bind(third_kernel, g), "third", [late, f32(8 * rest, nz), *[ys] * nmy],
        [turned, halo, rows, extra_rows, up, down, *sm], 50 * voxels,
    )
    grad = jnp.zeros((nx * ny, nz), jnp.float32)
    field, lined = [early, late_rows], []
    for step in (2, 1, 0):
        ym = both_matchings(ym, "gy", "gz")
        state = [extra, extra_late, mom if step else mom0]
        kept = [late_pops if step else first_pops, fluid]
        scratch = [pltpu.VMEM((Q * g.rows * ny, nz), jnp.float32)]
        args = [*field, *state, *kept, grad, *lined]
        if step:
            *field, grad = call(
                bind(inner_kernel, g, step), f"inner{step}", [full, late, flat], args, 400 * voxels, scratch=scratch
            )
            args = [*ym, *field, *state]
            ym = call(
                bind(edge_kernel, g, step, True), f"send{step}", [ys] * nmy, args, 20 * voxels,
                scratch=[pltpu.VMEM((Q * g.rows, nz), jnp.float32)] * 2,
            )
            up, down, grad = call(
                bind(edge_kernel, g, step, False), f"edge{step}", [lines, lines, flat], [*args, *kept, grad], 40 * voxels
            )
            lined = [up, down]
            continue
        part = f32(Q * nx, nz)
        whole, up, down, grad = call(
            bind(inner_kernel, g, step), f"inner{step}", [full, part, part, flat], args, 400 * voxels, scratch=scratch
        )
        args = [*ym, up, down, *state, *kept, grad, whole.reshape(Q * nx, ny, nz)]
        adjoint, grad = call(
            bind(edge_kernel, g, step, False), f"edge{step}", [f32(Q * nx, ny, nz), flat], args, 40 * voxels,
            {len(args) - 1: 0}, spaces=[*[pltpu.VMEM] * (len(args) - 1), pltpu.HBM], out_spaces=[pltpu.HBM, pltpu.VMEM],
            scratch=[pltpu.VMEM((Q * nx, nz), jnp.float32)] * 2 + [pltpu.SemaphoreType.DMA((2,))],
        )
    return adjoint.reshape(Q, nx, ny, nz), grad.reshape(nx, ny, nz)


def solution(mesh):
    return jax.shard_map(
        local,
        mesh=mesh,
        in_specs=(
            P(None, None, "gx", "gy", "gz"),
            P("gx", "gy", "gz"),
            P("gx", "gy", "gz"),
            P(None, "gx", "gy", "gz"),
        ),
        out_specs=(P(None, "gx", "gy", "gz"), P("gx", "gy", "gz")),
        check_vma=False,
    )
```

```python
import functools

import jax
import jax.numpy as jnp
import numpy as np
from jax import lax
from jax.experimental import pallas as pl
from jax.experimental.pallas import tpu as pltpu
from jax.sharding import PartitionSpec as P


STEPS = 3
DEPTH = STEPS
SLOTS = 8
Q = 27

VEL = np.array([[a, b, c] for a in (-1, 0, 1) for b in (-1, 0, 1) for c in (-1, 0, 1)])


def pop(cx, cy, cz):
    return 9 * (cx + 1) + 3 * (cy + 1) + cz + 1


CUT = 32

U1, SOLID = 30, 33
TRAVEL = 34


def reach(quantity, dim, toward):
    if quantity < Q:
        return DEPTH - 1 - int(VEL[quantity, dim]) * toward
    return 1 if U1 <= quantity < U1 + 3 else 2


def mirrored(quantity, dim):
    if quantity >= Q:
        return quantity
    c = [int(v) for v in VEL[quantity]]
    c[dim] = -c[dim]
    return pop(*c)


UPWARD = [(q, p) for q in range(TRAVEL) for p in range(1, reach(q, 0, 1) + 1)]
PARTS = (UPWARD[:CUT], UPWARD[CUT:])
LINES = [(q, p) for q, p in UPWARD if q < Q and VEL[q, 1]]


def swapped(value, axis, odd, spare):
    length = lax.axis_size(axis)
    wide = lax.axis_size(spare) if spare else 1
    pairs = []
    for i in range(length):
        for k in range(wide):
            j, m = ((i + 1 if i % 2 == 1 else i - 1) if odd else i ^ 1), k
            if not 0 <= j < length:
                j, m = (i, k ^ 1) if spare else (j % length, k)
            if j < length and m < wide:
                pairs.append((i * wide + k, j * wide + m))
    return lax.ppermute(value, (axis, spare) if spare else axis, pairs)


def both_matchings(messages, axis, spare):
    return [swapped(m, axis, k == 1, spare) for k, m in enumerate(messages)]


def matchings(axis):
    return 2 if lax.axis_size(axis) > 2 else 1


class Place:
    def __init__(self, axis):
        index = lax.axis_index(axis)
        self.even = lax.rem(index, 2) == 0
        self.lower = index > 0
        self.upper = index < lax.axis_size(axis) - 1

    def send(self, up, down):
        return jnp.where(self.even, up, down), jnp.where(self.even, down, up)

    def put(self, refs, here, up, down):
        for ref, value in zip(refs, self.send(up, down)):
            ref[here, :] = value

    def take(self, refs, here):
        first, second = refs[0][here, :], refs[-1][here, :]
        below = jnp.where(self.even, second, first)
        above = jnp.where(self.even, first, second)
        zero = jnp.zeros_like(first)
        return jnp.where(self.lower, below, zero), jnp.where(self.upper, above, zero)


class Shape:
    def __init__(self, nx, ny, nz):
        self.nx, self.ny, self.nz = nx, ny, nz
        self.rows = nz // SLOTS
        self.halo = nx + DEPTH
        if nx + 2 * DEPTH >= self.rows or nx * SLOTS * 2 > nz or nx < DEPTH or ny != 8 or self.rows % 8:
            raise ValueError("local block")

    def row(self, x):
        return x % self.rows

    def at(self, quantity, row):
        return pl.ds((quantity * self.rows + row) * self.ny, self.ny)

    def line(self, quantity, y):
        return pl.ds(quantity * self.rows * self.ny + y, self.rows, stride=self.ny)

    def raw(self, quantity, x):
        start = (quantity * self.nx + x) * self.ny
        if not isinstance(start, int):
            start = pl.multiple_of(start, self.ny)
        return pl.ds(start, self.ny)

    def raw_line(self, quantity, y):
        return pl.ds(quantity * self.nx * self.ny + y, self.nx, stride=self.ny)

    def late(self, quantity, row):
        return pl.ds((quantity * (self.rows - self.nx) + row - self.nx) * self.ny, self.ny)

    def late_line(self, quantity, y):
        count = self.rows - self.nx
        return pl.ds(quantity * count * self.ny + y, count, stride=self.ny)

    def tile(self, index):
        return pl.ds(index * self.ny, self.ny)


def lanes(g):
    return lax.broadcasted_iota(jnp.int32, (g.ny, g.nz), 1)


def roll(value, by, axis):
    size = value.shape[axis]
    if isinstance(by, int):
        by = by % size
        if by == 0:
            return value
    return pltpu.roll(value, by, axis)


def moments(load):
    total, my, mz = [], [], []
    for a in (-1, 0, 1):
        t, z = [], []
        for b in (-1, 0, 1):
            low, mid, high = (load(pop(a, b, c)) for c in (-1, 0, 1))
            t.append(low + mid + high)
            z.append(high - low)
        total.append(t[0] + t[1] + t[2])
        my.append(t[2] - t[0])
        mz.append(z[0] + z[1] + z[2])
    return (
        total[0] + total[1] + total[2],
        total[2] - total[0],
        my[0] + my[1] + my[2],
        mz[0] + mz[1] + mz[2],
    )


def velocity(load):
    rho, mx, my, mz = moments(load)
    inverse = 1.0 / rho
    return rho, mx * inverse, my * inverse, mz * inverse


def source(g, seed, mom, q, x):
    if q < Q:
        return seed[g.raw(q, x), :]
    return mom[g.raw({0: 1, 1: 5, 2: 8}[(q - Q) // 3] + (q - Q) % 3, x), :]


def open_kernel(g, seed_in, saved_in, porosity_in, fluid_in, seed, mom, saved, fluid, *refs):
    nx = g.nx
    *messages, porosity, sems = refs
    block = Q * nx * g.ny
    copies = [
        pltpu.make_async_copy(seed_in, seed, sems.at[0]),
        pltpu.make_async_copy(porosity_in, porosity, sems.at[1]),
        pltpu.make_async_copy(fluid_in, fluid, sems.at[2]),
        pltpu.make_async_copy(saved_in.at[pl.ds(2 * block, block), :], saved.at[pl.ds(0, block), :], sems.at[3]),
        pltpu.make_async_copy(saved_in.at[pl.ds(block, block), :], saved.at[pl.ds(block, block), :], sems.at[4]),
    ]
    for copy in copies:
        copy.start()
    lane = lanes(g)
    group, offset = lane // SLOTS, lane % SLOTS
    joint = []
    for q in range(TRAVEL):
        if q == 0:
            copies[0].wait()
        if q == Q:
            for copy in copies[1:]:
                copy.wait()

            def row(x, carry):
                here = g.raw(0, x)
                mom[g.raw(8, x), :] = jnp.where(fluid[here, :] == 1, porosity[here, :], 1.0)
                for part in range(2):
                    found = velocity(lambda i: saved[g.raw(part * Q + i, x), :])
                    for k in range(4):
                        mom[g.raw(4 * part + k, x), :] = found[k]
                return carry

            for x in range(nx):
                row(x, 0)
        half = (q % 2) * nx
        acc = joint.pop() if q % 2 else jnp.zeros((g.ny, g.nz), jnp.float32)
        for x in range(nx):
            moved = roll(source(g, seed, mom, q, x), (half + x) * SLOTS + DEPTH, 1)
            acc = jnp.where(group == half + x, moved, acc)
        joint.append(acc)
    z = Place("gz")
    if len(joint) % 2:
        joint.append(joint[-1])
    for k in range(len(joint) // 2):
        first, second = joint[2 * k], joint[2 * k + 1]
        up = jnp.where(offset < 4, first, roll(second, 4, 1))
        down = jnp.where(offset < 4, roll(first, -3, 1), roll(second, 1, 1))
        z.put(messages, g.tile(k), up, down)


def bulk_kernel(g, part, seed, mom, *messages):
    x = Place("gx")
    for k, (q, p) in enumerate(part):
        up, down = source(g, seed, mom, q, g.nx - p), source(g, seed, mom, mirrored(q, 0), p - 1)
        x.put(messages, g.tile(k), up, down)


def place_kernel(g, mom, saved_in, extra, mom0, saved, sem):
    nx = g.nx
    fetch = pltpu.make_async_copy(saved_in.at[pl.ds(0, Q * nx * g.ny), :], saved, sem)
    fetch.start()
    for x in range(nx):
        for k in range(3):
            extra[g.raw(k, x), :] = mom[g.raw(1 + k, x), :]
            extra[g.raw(3 + k, x), :] = mom[g.raw(5 + k, x), :]
        solid = mom[g.raw(8, x), :]
        extra[g.raw(6, x), :] = solid
        extra[g.raw(7, x), :] = 1.0 - solid
    fetch.wait()

    def row(x, carry):
        found = velocity(lambda i: saved[g.raw(i, x), :])
        for k in range(4):
            mom0[g.raw(k, x), :] = found[k]
        return carry

    lax.fori_loop(0, nx, row, 0)


def swap_edges(g, i, row, own, edge):
    lane = lax.broadcasted_iota(jnp.int32, own.shape, 1)
    cz = int(VEL[i, 2])
    if cz == 0:
        return own, edge
    slot = row * SLOTS
    if cz > 0:
        here, out, back = 0, slot + DEPTH + 2, slot + DEPTH
    else:
        here, out, back = g.nz - 1, slot + DEPTH - 1, slot + DEPTH + 1
    return (
        jnp.where(lane == here, roll(edge, here - out, 1), own),
        jnp.where(lane == back, roll(own, back - here, 1), edge),
    )


def edge_of(g, q):
    return g.ny - 1 if VEL[q, 1] < 0 else 0


def second_kernel(g, seed, *refs):
    nx = g.nx
    heard, halo, messages = refs[: matchings("gz")], refs[matchings("gz")], refs[matchings("gz") + 1 :]
    lane = lanes(g)
    group, offset = lane // SLOTS, lane % SLOTS
    z, x = Place("gz"), Place("gx")
    below, above = [], []
    for k in range(-(-TRAVEL // 4)):
        low, high = z.take(heard, g.tile(k))
        below.append(low)
        above.append(high)
    tiles = []
    for q in range(TRAVEL):
        at = (q % 2) * nx * SLOTS + (q // 2 % 2) * 4
        low = roll(below[q // 4], -at, 1)
        high = roll(above[q // 4], DEPTH + 2 - at, 1)
        tiles.append(jnp.where(group < nx, jnp.where(offset < 4, low, high), 0.0))
        halo[g.tile(q), :] = tiles[-1]
    width = DEPTH * SLOTS
    per = g.nz // width
    for k in range(-(-TRAVEL // per)):
        up = down = jnp.zeros((g.ny, g.nz), jnp.float32)
        for j in range(min(per, TRAVEL - k * per)):
            tile = tiles[k * per + j]
            part = (lane >= j * width) & (lane < (j + 1) * width)
            up = jnp.where(part, roll(tile, j * width - (nx - DEPTH) * SLOTS, 1), up)
            down = jnp.where(part, roll(tile, j * width, 1), down)
        x.put(messages, g.tile(k), up, down)
    first = -(-TRAVEL // per) * g.ny
    for k, (q, p) in enumerate(LINES):

        def line(i, row):
            return seed[pl.ds((i * nx + row) * g.ny + edge_of(g, i), 1), :]

        x.put(messages, pl.ds(first + k, 1), line(q, nx - p), line(mirrored(q, 0), p - 1))


def edges_kernel(g, seed, halo, field, turned, up, down):
    for i in range(Q):
        edge = halo[g.tile(i), :]
        for x in range(g.nx):
            own, edge = swap_edges(g, i, x, seed[g.raw(i, x), :], edge)
            field[g.raw(i, x), :] = own
        turned[g.tile(i), :] = edge
    for k in range(9):
        a, c = k // 3 - 1, k % 3 - 1
        here = pl.ds(k * g.nx, g.nx)
        up[here, :] = field[g.raw_line(pop(a, -1, c), g.ny - 1), :]
        down[here, :] = field[g.raw_line(pop(a, 1, c), 0), :]


def third_kernel(g, turned, halo, up, down, *refs):
    nx = g.nx
    heard, (full, *messages, lines) = refs[: matchings("gx")], refs[matchings("gx") :]
    x, y = Place("gx"), Place("gy")
    group = lanes(g) // SLOTS
    lower, upper = group >= g.rows - DEPTH, (group >= nx) & (group < nx + DEPTH)
    width = DEPTH * SLOTS
    per = g.nz // width
    for k in range(-(-TRAVEL // per)):
        low, high = x.take(heard, g.tile(k))
        for j in range(min(per, TRAVEL - k * per)):
            q = k * per + j
            tile = turned[g.tile(q), :] if q < Q else halo[g.tile(q), :]
            tile = jnp.where(lower, roll(low, (g.rows - DEPTH) * SLOTS - j * width, 1), tile)
            full[g.tile(q), :] = jnp.where(upper, roll(high, nx * SLOTS - j * width, 1), tile)
    first = -(-TRAVEL // per) * g.ny
    found = {}
    for k, (q, p) in enumerate(LINES):
        low, high = x.take(heard, pl.ds(first + k, 1))
        found[q, g.row(-p)] = low
        found[mirrored(q, 0), nx - 1 + p] = high
    late = g.rows - nx
    for i in range(Q):
        if not VEL[i, 1]:
            continue
        edge = full[pl.ds(i * g.ny + edge_of(g, i), 1), :]
        for row in range(nx, g.rows):
            if (i, row) in found:
                own, edge = swap_edges(g, i, row, found[i, row], edge)
                lines[pl.ds(i * late + row - nx, 1), :] = own
        lines[pl.ds(i * late + g.halo - nx, 1), :] = edge
    for k in range(9):
        a, c = k // 3 - 1, k % 3 - 1
        y.put(messages, pl.ds(k * g.rows, nx), up[pl.ds(k * nx, nx), :], down[pl.ds(k * nx, nx), :])
        sent = (lines[pl.ds(pop(a, b, c) * late, late), :] for b in (-1, 1))
        y.put(messages, pl.ds(k * g.rows + nx, late), *sent)


def rows_kernel(g, full, *refs):
    *heard, field, extra = refs
    heard = heard[: matchings("gx")], heard[matchings("gx") :]
    nx = g.nx
    x, z = Place("gx"), Place("gz")
    lane = lanes(g)
    group, offset = lane // SLOTS, lane % SLOTS
    rows = {}
    for part, messages in zip(PARTS, heard):
        for k, (q, p) in enumerate(part):
            low, high = x.take(messages, g.tile(k))
            rows[q, g.row(-p)] = low
            rows[mirrored(q, 0), nx - 1 + p] = high
    for q in range(TRAVEL):
        ref, index = (field, q) if q < Q else (extra, q - Q)
        edge = full[g.tile(q), :]
        for row in range(nx, g.rows):
            if (q, row) in rows:
                own = rows[q, row]
                if q < Q:
                    own, edge = swap_edges(g, q, row, own, edge)
                ref[g.late(index, row), :] = own
        ref[g.late(index, g.halo), :] = edge
    for p in (1, 2):
        for row, there in ((g.row(-p), x.lower), (nx - 1 + p, x.upper)):
            extra[g.late(7, row), :] = jnp.where(there, 1.0 - rows[SOLID, row], 0.0)
    lower, upper = group >= g.rows - DEPTH, (group >= nx) & (group < nx + DEPTH)
    there = jnp.where(lower, jnp.where(x.lower, 1, 0), jnp.where(upper, jnp.where(x.upper, 1, 0), 1))
    there = there * jnp.where(offset < 4, jnp.where(z.lower, 1, 0), jnp.where(z.upper, 1, 0))
    extra[g.late(7, g.halo), :] = jnp.where(there == 1, 1.0 - full[g.tile(SOLID), :], 0.0)


def pulled_moments(p):
    t = {}
    for a in (-1, 0, 1):
        s0, s1, s2 = [], [], []
        for b in (-1, 0, 1):
            low, mid, high = (p[pop(a, b, c)] for c in (-1, 0, 1))
            both = low + high
            s0.append(4.0 * mid + both)
            s1.append(high - low)
            s2.append(both)
        both = s0[0] + s0[2]
        t[a] = (
            4.0 * s0[1] + both,
            s0[2] - s0[0],
            both,
            4.0 * s1[1] + (s1[0] + s1[2]),
            s1[2] - s1[0],
            4.0 * s2[1] + (s2[0] + s2[2]),
        )
    both = [t[-1][k] + t[1][k] for k in range(6)]
    full = [4.0 * t[0][k] + both[k] for k in range(6)]
    m0, my, myy, mz, myz, mzz = full
    mx, mxx = t[1][0] - t[-1][0], both[0]
    mxy, mxz = t[1][1] - t[-1][1], t[1][3] - t[-1][3]
    return m0, mx, my, mz, mxx, myy, mzz, mxy, mxz, myz


def edge_moments(p, side):
    t = {}
    for a in (-1, 0, 1):
        low, mid, high = (p[pop(a, side, c)] for c in (-1, 0, 1))
        both = low + high
        t[a] = (4.0 * mid + both, high - low, both)
    both = [t[-1][k] + t[1][k] for k in range(3)]
    m0, mz, mzz = (4.0 * t[0][k] + both[k] for k in range(3))
    mx, mxz = t[1][0] - t[-1][0], t[1][1] - t[-1][1]
    if side > 0:
        return m0, mx, m0, mz, both[0], m0, mzz, mx, mxz, mz
    return m0, mx, -m0, mz, both[0], m0, mzz, -mx, mxz, -mz


def transposed(p, u, solid, fluidity, side=0):
    found = edge_moments(p, side) if side else pulled_moments(p)
    m0, mx, my, mz, mxx, myy, mzz, mxy, mxz, myz = found
    ux, uy, uz = u
    usq = ux * ux + uy * uy + uz * uz
    vx = mxx * ux + mxy * uy + mxz * uz
    vy = mxy * ux + myy * uy + myz * uz
    vz = mxz * ux + myz * uy + mzz * uz
    quad = ux * vx + uy * vy + uz * vz
    scale = fluidity * (1.6 / 216.0)
    kept = -0.6 * fluidity
    base = scale * (m0 + 1.5 * usq * m0 - 4.5 * quad)
    bx = scale * (3.0 * (mx - ux * m0) + 9.0 * vx)
    by = scale * (3.0 * (my - uy * m0) + 9.0 * vy)
    bz = scale * (3.0 * (mz - uz * m0) + 9.0 * vz)
    out = [None] * Q
    for a in (-1, 0, 1):
        ga = base + bx if a > 0 else (base - bx if a < 0 else base)
        for b in (-1, 0, 1):
            gb = ga + by if b > 0 else (ga - by if b < 0 else ga)
            for c in (-1, 0, 1):
                gc = gb + bz if c > 0 else (gb - bz if c < 0 else gb)
                i = pop(a, b, c)
                if not side or b == side:
                    gc = kept * p[i] + gc
                if not side or b == -side:
                    gc = solid * p[Q - 1 - i] + gc
                out[i] = gc
    flow = m0 * (1.0 - 1.5 * usq) + 3.0 * (ux * mx + uy * my + uz * mz) + 4.5 * quad
    return out, flow


def inner_kernel(g, step, early, late, extra, extra_late, mom, saved, fluid, grad, *refs):
    nx = g.nx
    base, part_at = 3 * (2 - step), (Q if step == 1 else 0)
    lines = refs[:2] if step < STEPS - 1 else None
    *outs, field = refs[2:] if lines else refs
    zero = jnp.zeros((g.rows, g.nz), jnp.float32)
    for i in range(Q):
        for row in range(g.rows):
            field[g.at(i, row), :] = early[g.raw(i, row), :] if row < nx else late[g.late(i, row), :]
        if VEL[i, 1] < 0:
            field[g.line(i, g.ny - 1), :] = zero
        elif lines:
            field[g.line(i, g.ny - 1), :] = lines[0][pl.ds(i * g.rows, g.rows), :]
        if VEL[i, 1] > 0:
            field[g.line(i, 0), :] = zero
        elif lines:
            field[g.line(i, 0), :] = lines[1][pl.ds(i * g.rows, g.rows), :]

    def part(k, row):
        return extra[g.raw(k, row), :] if row < nx else extra_late[g.late(k, row), :]

    def parts(row):
        return [part(k, row) for k in (base, base + 1, base + 2, 6, 7)]

    def pull(row):
        return [
            roll(
                roll(field[g.at(i, g.row(row + int(VEL[i, 0]))), :], -int(VEL[i, 2]), 1),
                -int(VEL[i, 1]),
                0,
            )
            for i in range(Q)
        ]

    if step:
        next_early, next_late, grad_out = outs
        p = [
            roll(
                roll(field[g.at(i, g.halo), :], -(SLOTS * int(VEL[i, 0]) + int(VEL[i, 2])), 1),
                -int(VEL[i, 1]),
                0,
            )
            for i in range(Q)
        ]
        *u, solid, fluidity = parts(g.halo)
        out, _ = transposed(p, u, solid, fluidity)
        for i in range(Q):
            next_late[g.late(i, g.halo), :] = out[i]
    else:
        result, up, down, grad_out = outs

    for x in range(-step, nx + step):
        row, local = g.row(x), 0 <= x < nx
        p = pull(row)
        if step:
            *u, solid, fluidity = parts(row)
        else:
            u = [mom[g.raw(1 + k, x), :] for k in range(3)]
            solid, fluidity = part(6, row), part(7, row)
        out, flow = transposed(p, u, solid, fluidity)
        if local:
            rho = mom[g.raw(4 * (2 - step) if step else 0, x), :]
            same = cross = None
            for i in range(Q):
                f = saved[g.raw(part_at + i, x), :]
                one, two = p[i] * f, p[Q - 1 - i] * f
                same, cross = (one, two) if same is None else (same + one, cross + two)
            term = 0.6 * same + cross - (1.6 / 216.0) * (rho * flow)
            here = g.tile(x)
            grad_out[here, :] = jnp.where(fluid[here, :] == 1, grad[here, :] + term, 0.0)
        for i in range(Q):
            if step:
                here = g.late(i, g.halo)
                own, edge = swap_edges(g, i, row, out[i], next_late[here, :])
                if VEL[i, 2]:
                    next_late[here, :] = edge
                if row < nx:
                    next_early[g.raw(i, row), :] = own
                else:
                    next_late[g.late(i, row), :] = own
            else:
                result[g.raw(i, x), :] = out[i]
    if not step:
        for i in range(Q):
            here = pl.ds(i * nx, nx)
            up[here, :] = result[g.raw_line(i, g.ny - 1), :]
            down[here, :] = result[g.raw_line(i, 0), :]


def edge_kernel(g, step, sending, *refs):
    nx = g.nx
    y = Place("gy")
    base = 3 * (2 - step)
    sub = lax.broadcasted_iota(jnp.int32, (g.rows, g.nz), 0)
    lane = lax.broadcasted_iota(jnp.int32, (g.rows, g.nz), 1)
    part_at = Q if step == 1 else 0
    heard, refs = refs[: matchings("gy")], refs[matchings("gy") :]
    early, late, extra, extra_late, mom, *refs = refs
    if sending:
        *messages, up, down = refs
    elif step:
        saved, fluid, grad_in, up, down, grad = refs
    else:
        saved, fluid, grad_in, _, whole, grad, up, down, sems = refs
    if not sending:
        grad[...] = grad_in[...]

    def wanted(side):
        return [i for i in range(Q) if not sending or VEL[i, 1] == -side]

    def joined(first, second, k, edge):
        return jnp.concatenate([first[g.raw_line(k, edge), :], second[g.late_line(k, edge), :]], axis=0)

    def swapped_edges(i, tile):
        cz = int(VEL[i, 2])
        here, out, back = (0, DEPTH + 2, DEPTH) if cz > 0 else (g.nz - 1, DEPTH - 1, DEPTH + 1)
        own = jnp.broadcast_to(tile[:, here : here + 1], tile.shape)
        edge = jnp.broadcast_to(tile[g.halo : g.halo + 1, :], tile.shape)
        column = jnp.sum(jnp.where(lane == sub * SLOTS + out, edge, 0.0), axis=1, keepdims=True)
        line = jnp.sum(jnp.where(lane == sub * SLOTS + back, own, 0.0), axis=0, keepdims=True)
        tile = jnp.where((lane == here) & (sub != g.halo), column, tile)
        return jnp.where((sub == g.halo) & (lane % SLOTS == back), line, tile)

    def before(i, side):
        if step:
            return joined(early, late, i, g.ny - 1 if side > 0 else 0)
        return (early if side > 0 else late)[pl.ds(i * nx, nx), :]

    def store(side, i, value):
        count = g.rows if step else nx
        (up if side > 0 else down)[pl.ds(i * count, count), :] = value

    def correct(side):
        edge = g.ny - 1 if side > 0 else 0
        p = [None] * Q
        for k in range(9):
            a, c = k // 3 - 1, k % 3 - 1
            here = pl.ds(k * g.rows, g.rows)
            first, second = heard[0][here, :], heard[-1][here, :]
            value = jnp.where(y.even if side > 0 else jnp.logical_not(y.even), first, second)
            moved = roll(roll(value, -a, 0), -c, 1)
            if step:
                moved = jnp.where(sub == g.halo, roll(value, -(SLOTS * a + c), 1), moved)
            else:
                moved = moved[:nx]
            p[pop(a, side, c)] = moved
        if step:
            *u, solid, fluidity = (joined(extra, extra_late, k, edge) for k in (base, base + 1, base + 2, 6, 7))
        else:
            u = [mom[g.raw_line(1 + k, edge), :] for k in range(3)]
            solid, fluidity = (extra[g.raw_line(k, edge), :] for k in (6, 7))
        out, flow = transposed(p, u, solid, fluidity, side)
        for i in wanted(side):
            tile = swapped_edges(i, out[i]) if step and VEL[i, 2] else out[i]
            store(side, i, before(i, side) + tile)
        if sending:
            return
        rho = mom[g.raw_line(4 * (2 - step) if step else 0, edge), :]
        same = cross = None
        for i in range(Q):
            if VEL[i, 1] != side:
                continue
            value = p[i][:nx]
            one = value * saved[g.raw_line(part_at + i, edge), :]
            two = value * saved[g.raw_line(part_at + Q - 1 - i, edge), :]
            same, cross = (one, two) if same is None else (same + one, cross + two)
        term = 0.6 * same + cross - (1.6 / 216.0) * (rho * flow[:nx])
        at = g.raw_line(0, edge)
        grad[at, :] = jnp.where(fluid[at, :] == 1, grad_in[at, :] + term, 0.0)

    def write(side):
        edge = g.ny - 1 if side > 0 else 0
        return pltpu.make_async_copy(up if side > 0 else down, whole.at[:, edge, :], sems.at[0 if side > 0 else 1])

    for side, there in ((1, y.upper), (-1, y.lower)):

        @pl.when(there)
        def _(side=side):
            correct(side)
            if not step:
                write(side).start()

        if step:

            @pl.when(jnp.logical_not(there))
            def _(side=side):
                for i in wanted(side):
                    store(side, i, before(i, side))

    if sending:
        for k in range(9):
            a, c = k // 3 - 1, k % 3 - 1
            here = pl.ds(k * g.rows, g.rows)
            sent = (up, pop(a, -1, c)), (down, pop(a, 1, c))
            y.put(messages, here, *(ref[pl.ds(i * g.rows, g.rows), :] for ref, i in sent))
    elif not step:
        for side, there in ((1, y.upper), (-1, y.lower)):

            @pl.when(there)
            def _(side=side):
                write(side).wait()


def call(kernel, outs, args, flops, aliases=None, scratch=(), spaces=None, out_spaces=None):
    moved = 4 * sum(int(np.prod(a.shape)) for a in [*args, *outs])
    spaces = spaces or [pltpu.VMEM] * len(args)
    out_spaces = out_spaces or [pltpu.VMEM] * len(outs)
    return pl.pallas_call(
        kernel,
        out_shape=outs,
        in_specs=[pl.BlockSpec(memory_space=m) for m in spaces],
        out_specs=[pl.BlockSpec(memory_space=m) for m in out_spaces],
        scratch_shapes=scratch,
        input_output_aliases=aliases or {},
        compiler_params=pltpu.CompilerParams(vmem_limit_bytes=VMEM_LIMIT),
        cost_estimate=pl.CostEstimate(flops=flops, bytes_accessed=moved, transcendentals=0),
    )(*args)


VMEM_LIMIT = 24 * 1024 * 1024


def local(saved, porosity, fluid, seed_adjoint):
    nx, ny, nz = porosity.shape
    g = Shape(nx, ny, nz)
    bind = functools.partial
    f32 = lambda *shape: jax.ShapeDtypeStruct(shape, jnp.float32)
    seed = seed_adjoint.reshape(Q * nx * ny, nz)
    pops = saved.reshape(STEPS * Q * nx * ny, nz)
    porosity = porosity.reshape(nx * ny, nz)
    fluid = fluid.reshape(nx * ny, nz)
    voxels, rest = nx * ny * nz, (g.rows - nx) * ny
    flat, full, late = f32(nx * ny, nz), f32(Q * nx * ny, nz), f32(Q * rest, nz)
    zs = f32(-(-TRAVEL // 4) * ny, nz)
    xs = [f32(len(part) * ny, nz) for part in PARTS]
    ss = f32((-(-TRAVEL // (nz // (DEPTH * SLOTS))) - (-len(LINES) // ny)) * ny, nz)
    ys, yl, lines = f32(9 * g.rows, nz), f32(9 * nx, nz), f32(Q * g.rows, nz)

    hbm = lambda *values: [pltpu.with_memory_space_constraint(v, pltpu.HBM) for v in values]
    nmx, nmy, nmz = (matchings(axis) for axis in ("gx", "gy", "gz"))
    seed, mom, late_pops, fluid, *zm = call(
        bind(open_kernel, g),
        [full, f32(9 * nx * ny, nz), f32(2 * Q * nx * ny, nz), jax.ShapeDtypeStruct((nx * ny, nz), jnp.int32), *[zs] * nmz],
        hbm(seed, pops, porosity, fluid), 200 * voxels, spaces=[pltpu.HBM] * 4,
        scratch=[pltpu.VMEM((nx * ny, nz), jnp.float32), pltpu.SemaphoreType.DMA((5,))],
    )
    zm = both_matchings(zm, "gz", None)
    xm0 = call(bind(bulk_kernel, g, PARTS[0]), [xs[0]] * nmx, [seed, mom], 10 * voxels)
    xm0 = both_matchings(xm0, "gx", "gz")
    extra, mom0, first_pops = call(
        bind(place_kernel, g), [f32(8 * nx * ny, nz), f32(4 * nx * ny, nz), full],
        [mom, *hbm(pops)], 50 * voxels, spaces=[pltpu.VMEM, pltpu.HBM], scratch=[pltpu.SemaphoreType.DMA(())],
    )
    halo, *sm = call(bind(second_kernel, g), [f32(TRAVEL * ny, nz), *[ss] * nmx], [seed, *zm], 20 * voxels)
    sm = both_matchings(sm, "gx", "gz")
    xm1 = call(bind(bulk_kernel, g, PARTS[1]), [xs[1]] * nmx, [seed, mom], 10 * voxels)
    xm1 = both_matchings(xm1, "gx", "gz")
    early, turned, up, down = call(bind(edges_kernel, g), [full, f32(Q * ny, nz), yl, yl], [seed, halo], 50 * voxels)
    whole, *ym = call(
        bind(third_kernel, g), [f32(TRAVEL * ny, nz), *[ys] * nmy],
        [turned, halo, up, down, *sm], 20 * voxels, scratch=[pltpu.VMEM((Q * (g.rows - nx), nz), jnp.float32)],
    )
    late_rows, extra_late = call(bind(rows_kernel, g), [late, f32(8 * rest, nz)], [whole, *xm0, *xm1], 50 * voxels)
    grad = jnp.zeros((nx * ny, nz), jnp.float32)
    field, lined = [early, late_rows], []
    for step in (2, 1, 0):
        ym = both_matchings(ym, "gy", "gz")
        state = [extra, extra_late, mom if step else mom0]
        kept = [late_pops if step else first_pops, fluid]
        scratch = [pltpu.VMEM((Q * g.rows * ny, nz), jnp.float32)]
        args = [*field, *state, *kept, grad, *lined]
        if step:
            *field, grad = call(bind(inner_kernel, g, step), [full, late, flat], args, 400 * voxels, scratch=scratch)
            args = [*ym, *field, *state]
            ym = call(
                bind(edge_kernel, g, step, True), [ys] * nmy, args, 20 * voxels,
                scratch=[pltpu.VMEM((Q * g.rows, nz), jnp.float32)] * 2,
            )
            up, down, grad = call(
                bind(edge_kernel, g, step, False), [lines, lines, flat], [*args, *kept, grad], 40 * voxels
            )
            lined = [up, down]
            continue
        part = f32(Q * nx, nz)
        whole, up, down, grad = call(
            bind(inner_kernel, g, step), [full, part, part, flat], args, 400 * voxels, scratch=scratch
        )
        args = [*ym, up, down, *state, *kept, grad, whole.reshape(Q * nx, ny, nz)]
        adjoint, grad = call(
            bind(edge_kernel, g, step, False), [f32(Q * nx, ny, nz), flat], args, 40 * voxels,
            {len(args) - 1: 0}, spaces=[*[pltpu.VMEM] * (len(args) - 1), pltpu.HBM], out_spaces=[pltpu.HBM, pltpu.VMEM],
            scratch=[pltpu.VMEM((Q * nx, nz), jnp.float32)] * 2 + [pltpu.SemaphoreType.DMA((2,))],
        )
    return adjoint.reshape(Q, nx, ny, nz), grad.reshape(nx, ny, nz)


def solution(mesh):
    return jax.shard_map(
        local,
        mesh=mesh,
        in_specs=(
            P(None, None, "gx", "gy", "gz"),
            P("gx", "gy", "gz"),
            P("gx", "gy", "gz"),
            P(None, "gx", "gy", "gz"),
        ),
        out_specs=(P(None, "gx", "gy", "gz"), P("gx", "gy", "gz")),
        check_vma=False,
    )
```
